256 devices in a mesh: seq: 32 (over x, z), ch: 8 (over y, core).
Axes of the slice: x: 4, y: 4, z: 8, core: 2. Of those that a mesh axis runs over, the one named last changes fastest.
Arguments:
- queries_in: bfloat16 [8192, 8192], P('seq', 'ch'), may hold values from -160 to 160
- keys_in: bfloat16 [8192, 8192], P('seq', 'ch'), may hold values from -8 to 8
- values_in: bfloat16 [8192, 8192], P('seq', 'ch'), may hold values from -6 to 6
- gate_branch: bfloat16 [8192, 8192], P('seq', 'ch'), may hold values from -6 to 6
- key_branch: bfloat16 [8192, 8192], P('seq', 'ch'), may hold values from -6 to 6
- mr_filter: bfloat16 [128, 8192], P(None, 'ch'), may hold values from -3 to 3
- out_grad: bfloat16 [8192, 8192], P('seq', 'ch'), may hold values from -40 to 40
- doc_ids: int32 [8192], replicated, may hold values from 0 to 63, never falling along the last dimension, each value on 1 to 1024 neighbouring positions
Outputs:
- query_grad: bfloat16 [8192, 8192], P('seq', 'ch')
- key_grad: bfloat16 [8192, 8192], P('seq', 'ch')
- value_grad: bfloat16 [8192, 8192], P('seq', 'ch')
- gate_grad: bfloat16 [8192, 8192], P('seq', 'ch')
- branch_grad: bfloat16 [8192, 8192], P('seq', 'ch')
- filter_step: float32 [128, 8192], P('seq', 'ch')
The draws below stay inside these ranges and needn't reach their ends.
Inputs may be any that keep to these rules, and one draw needn't show every extreme that they name: `doc_ids`: document numbers never fall along the sequence; each document has 1 to 1024 tokens and one has exactly 1024.
All inputs are finite; a program needn't handle non-finite values.
Results may differ from the reference program's by a relative error of at most 0.009.
Values may be sent and summed in bfloat16 or wider, within the bound.
No kernel may reach another device: no remote copies, remote signals or barrier semaphores. Data moves between devices by JAX's collectives and lax.ppermute only.
A program may use at most 128 MiB of HBM per device.

```python
import math
import jax
import jax.numpy as jnp
import numpy as np
from jax import lax

D = 8192
HD = 128
TAPS = 128
TOK_DEV = 256
SPAN = 4
HEADS = 64
TOKENS = 8192
MOST = 1024
DOCS = 64
N_SEQ = 32


def attention_pair(key):
    base = jax.random.fold_in(key, 11)
    query_key, key_key = jax.random.split(base, 2)
    key_rows = jax.random.normal(key_key, (TOKENS, D), jnp.float32)
    query_rows = jax.random.normal(query_key, (TOKENS, D), jnp.float32)
    return (query_rows, key_rows)


def draw_queries_in(key, part):
    return attention_pair(key)[0].astype(jnp.bfloat16)


def draw_keys_in(key, part):
    return attention_pair(key)[1].astype(jnp.bfloat16)


def draw_out_grad(key, part):
    first, second = jax.random.split(jax.random.fold_in(key, 23))
    channel = jnp.arange(D, dtype=jnp.float32) / (D - 1)
    spread = jnp.exp(jax.random.uniform(second, (D,), jnp.float32, 0.0, math.log(10.0))) / 3.0
    values = jnp.clip(jax.random.normal(first, (TOKENS, D), jnp.float32), -6.0, 6.0)
    rising = jnp.exp(math.log(3.0) * channel) / 1.7
    return (values * spread[None, :] * rising[None, :]).astype(jnp.bfloat16)


def draw_mr_filter(key, part):
    first = jax.random.fold_in(key, 37)
    channel = jnp.arange(D, dtype=jnp.float32) / (D - 1)
    values = 0.15 * jnp.clip(jax.random.normal(first, (TAPS, D), jnp.float32), -6.0, 6.0)
    rising = jnp.exp(math.log(3.0) * channel)
    return (values * rising[None, :]).astype(jnp.bfloat16)


def steps_of(stream_key, dims, shards, least, high):
    loudness = 1.0
    for axis_at, blocks in shards:
        steps = jax.random.uniform(jax.random.fold_in(jax.random.fold_in(stream_key, 6), axis_at), (blocks,), jnp.float32, least / len(shards), high / len(shards))
        loudness = loudness * jnp.repeat(jnp.exp(steps), dims[axis_at] // blocks).reshape((-1,) + (1,) * (len(dims) - 1 - axis_at))
    return loudness


def profile(amount, total, bound, lean):
    loads = [(1 << 20) // math.isqrt(rank ** lean) + 1 for rank in range(2, amount + 1)]
    spare, counts = total - bound - (amount - 1), [1] * (amount - 1)
    while spare > 0:
        movable = [i for i in range(amount - 1) if counts[i] < bound]
        mass, remaining = sum([loads[i] for i in movable]), spare
        for i in movable:
            more = min(bound - counts[i], max(1, remaining * loads[i] // mass), spare)
            counts[i] = counts[i] + more
            spare = spare - more
    return np.array([bound] + counts)


def ragged_sizes(stream_key, count, total, most, slope):
    if count == 2:
        one = jax.random.randint(stream_key, (), max(1, total - most), min(most, total - 1) + 1)
        return jnp.stack([one, total - one])
    tallies = jnp.asarray(profile(count, total, most, slope), jnp.int32)
    pairs = (count - 1) // 2
    donor, receiver = tallies[1:1 + 2 * pairs:2], tallies[2:2 + 2 * pairs:2]
    room = jnp.minimum(donor - 1, most - receiver)
    shifted = jax.random.randint(jax.random.fold_in(stream_key, 1), (pairs,), 0, 1 << 20) % (room + 1)
    tallies = tallies.at[1:1 + 2 * pairs:2].set(donor - shifted).at[2:2 + 2 * pairs:2].set(receiver + shifted)
    return tallies[jax.random.permutation(jax.random.fold_in(stream_key, 2), count)]


def noise(own_key, extent, deviation, bound, pieces=(), kind=jnp.bfloat16):
    loudness = steps_of(own_key, extent, pieces, -0.22, 0.18) if pieces else 1.0
    values = jax.random.normal(own_key, extent, jnp.float32) * deviation * loudness
    return jnp.minimum(jnp.maximum(values, -bound), bound).astype(kind)


def setup_inputs(seed: int = 0) -> dict:
    streams_of = jax.random.split(jax.random.key(seed), 9)
    queries_in = draw_queries_in(jax.random.fold_in(streams_of[8], 71), 0)
    keys_in = draw_keys_in(jax.random.fold_in(streams_of[8], 71), 0)
    values_in = noise(streams_of[2], (TOKENS, D), 1.0, 6.0, ((0, 32), (1, 8)))
    gate_branch = noise(streams_of[3], (TOKENS, D), 1.0, 6.0, ((0, 32), (1, 8)))
    key_branch = noise(streams_of[4], (TOKENS, D), 1.0, 6.0, ((0, 32), (1, 8)))
    mr_filter = draw_mr_filter(jax.random.fold_in(streams_of[8], 71), 0)
    out_grad = draw_out_grad(jax.random.fold_in(streams_of[8], 71), 0)
    doc_ids = jnp.searchsorted(jnp.cumsum(ragged_sizes(streams_of[7], DOCS, TOKENS, MOST, 2)), jnp.arange(TOKENS), side="right").astype(jnp.int32)
    return dict(queries_in=queries_in, keys_in=keys_in, values_in=values_in, gate_branch=gate_branch, key_branch=key_branch, mr_filter=mr_filter, out_grad=out_grad, doc_ids=doc_ids)


def causal_conv(extended, weights_in):
    rows = extended.shape[0] - (TAPS - 1)

    def add_tap(tap, total):
        index = jnp.asarray(tap).astype(jnp.int32)
        piece = lax.dynamic_slice_in_dim(extended, (TAPS - 1 - index).astype(jnp.int32), rows, 0).astype(jnp.float32)
        weight_row = lax.dynamic_index_in_dim(weights_in, index, 0, keepdims=False).astype(jnp.float32)
        return total + weight_row[None, :] * piece
    return lax.fori_loop(0, TAPS, add_tap, jnp.zeros((rows, extended.shape[1]), jnp.float32))

def anti_conv(extended, weights_in):
    rows = extended.shape[0] - (TAPS - 1)

    def add_tap(tap, total):
        index = jnp.asarray(tap).astype(jnp.int32)
        piece = lax.dynamic_slice_in_dim(extended, index, rows, 0).astype(jnp.float32)
        weight_row = lax.dynamic_index_in_dim(weights_in, index, 0, keepdims=False).astype(jnp.float32)
        return total + weight_row[None, :] * piece
    return lax.fori_loop(0, TAPS, add_tap, jnp.zeros((rows, extended.shape[1]), jnp.float32))

def filter_corr(extended, gradient):
    rows = gradient.shape[0]
    grad_float = gradient.astype(jnp.float32)

    def one_tap(tap):
        piece = lax.dynamic_slice_in_dim(extended, (TAPS - 1 - tap).astype(jnp.int32), rows, 0).astype(jnp.float32)
        return lax.optimization_barrier(jnp.sum(grad_float * piece, 0))
    return lax.map(one_tap, jnp.arange(TAPS, dtype=jnp.int32))

def reference(queries_in, keys_in, values_in, gate_branch, key_branch, mr_filter, out_grad, doc_ids):
    window = (SPAN + 1) * TOK_DEV
    score_scale = HD ** (-0.5)
    front = jnp.zeros((SPAN * TOK_DEV, D), jnp.bfloat16)
    key_pad = jnp.concatenate([front, keys_in], 0)
    value_pad = jnp.concatenate([front, values_in], 0)
    doc_pad = jnp.concatenate([jnp.full((SPAN * TOK_DEV,), -1, jnp.int32), doc_ids], 0)
    blocks = jnp.arange(N_SEQ, dtype=jnp.int32)

    def block_scores(block):
        start = (block * TOK_DEV).astype(jnp.int32)
        query_rows = lax.dynamic_slice_in_dim(queries_in, start, TOK_DEV, 0).astype(jnp.float32).reshape(TOK_DEV, HEADS, HD)
        key_rows = lax.dynamic_slice_in_dim(key_pad, start, window, 0).astype(jnp.float32).reshape(window, HEADS, HD)
        value_rows = lax.dynamic_slice_in_dim(value_pad, start, window, 0).astype(jnp.float32).reshape(window, HEADS, HD)
        query_doc = lax.dynamic_slice_in_dim(doc_ids, start, TOK_DEV, 0)
        key_doc = lax.dynamic_slice_in_dim(doc_pad, start, window, 0)
        query_pos = start + jnp.arange(TOK_DEV, dtype=jnp.int32)
        key_pos = start - SPAN * TOK_DEV + jnp.arange(window, dtype=jnp.int32)
        allowed = (query_doc[:, None] == key_doc[None, :]) & (key_pos[None, :] <= query_pos[:, None])
        scores = jnp.einsum('qhd,khd->hqk', query_rows, key_rows) * score_scale
        scores = jnp.where(allowed[None], scores, -jnp.inf)
        return (scores, allowed, query_rows, key_rows, value_rows)

    def forward(block):
        scores, allowed, query_rows, key_rows, value_rows = block_scores(block)
        row_max = lax.optimization_barrier(jnp.max(scores, -1))
        log_total = row_max + jnp.log(lax.optimization_barrier(jnp.sum(jnp.exp(scores - row_max[..., None]), -1)))
        weights = jnp.where(allowed[None], jnp.exp(scores - log_total[..., None]), 0.0)
        probs = weights.astype(jnp.bfloat16)
        output = jnp.einsum('hqk,khd->qhd', probs.astype(jnp.float32), value_rows)
        return (output.astype(jnp.bfloat16).reshape(TOK_DEV, D), log_total)
    attn_blocks, totals = lax.map(forward, blocks)
    attn_out = attn_blocks.reshape(TOKENS, D)
    mixed = (key_branch.astype(jnp.float32) * attn_out.astype(jnp.float32)).astype(jnp.bfloat16)
    mixed_ext = jnp.concatenate([jnp.zeros((TAPS - 1, D), jnp.bfloat16), mixed], 0)
    conv_out = causal_conv(mixed_ext, mr_filter)
    gate_grad = (out_grad.astype(jnp.float32) * conv_out).astype(jnp.bfloat16)
    conv_grad = (out_grad.astype(jnp.float32) * gate_branch.astype(jnp.float32)).astype(jnp.bfloat16)
    grad_ext = jnp.concatenate([conv_grad, jnp.zeros((TAPS - 1, D), jnp.bfloat16)], 0)
    mixed_grad = anti_conv(grad_ext, mr_filter)
    filter_grad = filter_corr(mixed_ext, conv_grad)
    branch_grad = (mixed_grad * attn_out.astype(jnp.float32)).astype(jnp.bfloat16)
    attn_grad = (mixed_grad * key_branch.astype(jnp.float32)).astype(jnp.bfloat16)

    def backward(carry, inputs):
        key_acc, value_acc = carry
        block, log_total = inputs
        start = (block * TOK_DEV).astype(jnp.int32)
        scores, allowed, query_rows, key_rows, value_rows = block_scores(block)
        weights = jnp.where(allowed[None], jnp.exp(scores - log_total[..., None]), 0.0)
        probs = weights.astype(jnp.bfloat16).astype(jnp.float32)
        grad_rows = lax.dynamic_slice_in_dim(attn_grad, start, TOK_DEV, 0).astype(jnp.float32).reshape(TOK_DEV, HEADS, HD)
        out_rows = lax.dynamic_slice_in_dim(attn_out, start, TOK_DEV, 0).astype(jnp.float32).reshape(TOK_DEV, HEADS, HD)
        row_dot = jnp.einsum('qhd,qhd->hq', grad_rows, out_rows)
        prob_grad = jnp.einsum('qhd,khd->hqk', grad_rows, value_rows)
        score_grad = (weights * (prob_grad - row_dot[..., None])).astype(jnp.bfloat16).astype(jnp.float32)
        query_part = (jnp.einsum('hqk,khd->qhd', score_grad, key_rows) * score_scale).astype(jnp.bfloat16).reshape(TOK_DEV, D)
        key_terms = (jnp.einsum('hqk,qhd->khd', score_grad, query_rows) * score_scale).reshape(window, D)
        value_terms = jnp.einsum('hqk,qhd->khd', probs, grad_rows).reshape(window, D)
        key_acc = lax.dynamic_update_slice_in_dim(key_acc, lax.dynamic_slice_in_dim(key_acc, start, window, 0) + key_terms, start, 0)
        value_acc = lax.dynamic_update_slice_in_dim(value_acc, lax.dynamic_slice_in_dim(value_acc, start, window, 0) + value_terms, start, 0)
        return ((key_acc, value_acc), query_part)
    empty = jnp.zeros(((N_SEQ + SPAN) * TOK_DEV, D), jnp.float32)
    (key_acc, value_acc), query_parts = lax.scan(backward, (empty, empty), (blocks, totals))
    query_grad = query_parts.reshape(TOKENS, D)
    key_grad = key_acc[SPAN * TOK_DEV:].astype(jnp.bfloat16)
    value_grad = value_acc[SPAN * TOK_DEV:].astype(jnp.bfloat16)
    filter_sq = jnp.sum(jnp.square(mr_filter.astype(jnp.float32)))
    trust = jnp.sqrt(filter_sq) / jnp.sqrt(jnp.sum(filter_grad * filter_grad) + 1e-06)
    filter_step = trust * filter_grad
    return (query_grad, key_grad, value_grad, gate_grad, branch_grad, filter_step)
```

```python
import jax
import jax.numpy as jnp
from jax import lax
from jax.experimental import pallas as pl
from jax.experimental.pallas import tpu as pltpu
from jax.sharding import PartitionSpec as P


HD = 128
TAPS = 128
SPAN = 4
ROW = 8
TOK = 256
NEG = -1e30
STEP = 4
SCALE = HD ** (-0.5)


def causal_conv(extended, weights_in):
    kernel = jnp.flip(weights_in, 0)[:, None, :]
    return lax.conv_general_dilated(
        extended[None],
        kernel,
        (1,),
        "VALID",
        dimension_numbers=("NWC", "WIO", "NWC"),
        feature_group_count=extended.shape[1],
        preferred_element_type=jnp.float32,
    )[0]


def anti_conv(extended, weights_in):
    return lax.conv_general_dilated(
        extended[None],
        weights_in[:, None, :],
        (1,),
        "VALID",
        dimension_numbers=("NWC", "WIO", "NWC"),
        feature_group_count=extended.shape[1],
        preferred_element_type=jnp.float32,
    )[0]


def pack_kernel(*refs):
    *in_refs, out_ref = refs
    for head in range(out_ref.shape[0]):
        for n, in_ref in enumerate(in_refs):
            out_ref[head, n * TOK : (n + 1) * TOK] = in_ref[:, head * HD : (head + 1) * HD]


def pack(*arrays):
    heads = arrays[0].shape[1] // HD
    n = len(arrays)
    return pl.pallas_call(
        pack_kernel,
        grid=(heads // STEP,),
        in_specs=[pl.BlockSpec((TOK, STEP * HD), lambda h: (0, h))] * n,
        out_specs=pl.BlockSpec((STEP, n * TOK, HD), lambda h: (h, 0, 0)),
        out_shape=jax.ShapeDtypeStruct((heads, n * TOK, HD), arrays[0].dtype),
        name="pack",
    )(*arrays)


def pack_grad_kernel(q_ref, mixed_grad_ref, key_ref, out_ref):
    attn_grad = mixed_grad_ref[...] * key_ref[...].astype(jnp.float32)
    attn_grad = attn_grad.astype(jnp.bfloat16)
    for head in range(out_ref.shape[0]):
        lanes = slice(head * HD, (head + 1) * HD)
        out_ref[head, :TOK] = q_ref[:, lanes]
        out_ref[head, TOK:] = attn_grad[:, lanes]


def pack_grad(q, mixed_grad, key):
    heads = key.shape[1] // HD
    return pl.pallas_call(
        pack_grad_kernel,
        grid=(heads // STEP,),
        in_specs=[pl.BlockSpec((TOK, STEP * HD), lambda h: (0, h))] * 3,
        out_specs=pl.BlockSpec((STEP, 2 * TOK, HD), lambda h: (h, 0, 0)),
        out_shape=jax.ShapeDtypeStruct((heads, 2 * TOK, HD), key.dtype),
        name="pack_grad",
    )(q, mixed_grad, key)


def unpack_kernel(x_ref, *out_refs):
    for head in range(x_ref.shape[0]):
        for n, out_ref in enumerate(out_refs):
            out_ref[:, head * HD : (head + 1) * HD] = x_ref[head, n * TOK : (n + 1) * TOK]


def unpack(x):
    heads, rows, _ = x.shape
    n = rows // TOK
    return pl.pallas_call(
        unpack_kernel,
        grid=(heads // STEP,),
        in_specs=[pl.BlockSpec((STEP, rows, HD), lambda h: (h, 0, 0))],
        out_specs=[pl.BlockSpec((TOK, STEP * HD), lambda h: (0, h))] * n,
        out_shape=[jax.ShapeDtypeStruct((TOK, heads * HD), x.dtype)] * n,
        name="unpack",
    )(x)


def dot_nn(a, b):
    return jnp.dot(a, b, preferred_element_type=jnp.float32)


def window_of(block, width):
    first = block + (SPAN + 1 - width)
    return first, pl.ds(pl.multiple_of(first * TOK, TOK), width * TOK)


def key_blocks(kv_ref, kvh_ref):
    for b in range(SPAN + ROW):
        src = kvh_ref if b < SPAN else kv_ref
        at = b if b < SPAN else b - SPAN
        yield b, slice(b * TOK, (b + 1) * TOK), src[at, :TOK], src[at, TOK:]


def masked_scores(k, q, kdoc, qdoc, width):
    scores = dot_nn(k, q.T)
    same = jnp.concatenate([kdoc, kdoc], 1) == qdoc
    key_at = lax.broadcasted_iota(jnp.int32, scores.shape, 0)
    query_at = lax.broadcasted_iota(jnp.int32, scores.shape, 1) + (width - 1) * TOK
    return jnp.where(same & (key_at <= query_at), scores, NEG)


def by_width(width_ref, block, attend):
    for width in range(1, SPAN + 2):
        pl.when(width_ref[block] == width)(lambda width=width: attend(width))


def fwd_kernel(
    width_ref, kv_ref, kvh_ref, kdoc_ref, qdoc_ref, qg_ref, out_ref, top_ref, inv_ref, k_s, vt_s
):
    block = pl.program_id(0)

    @pl.when(block == 0)
    def _():
        for b, rows, k, v in key_blocks(kv_ref, kvh_ref):
            k_s[rows] = k
            vt_s[b] = v.T

    def attend(width):
        first, rows = window_of(block, width)
        q = qg_ref[0, :TOK]
        vt = jnp.concatenate([vt_s[first + n] for n in range(width)], 1)
        scores = masked_scores(k_s[rows], q, kdoc_ref[rows], qdoc_ref[0], width)
        top = jnp.max(scores, 0, keepdims=True)
        weights = jnp.exp((scores - top) * SCALE)
        inv = 1.0 / jnp.sum(weights, 0, keepdims=True)
        top_ref[0] = top
        inv_ref[0] = inv
        probs = (weights * inv).astype(jnp.bfloat16)
        out_ref[0] = dot_nn(vt, probs).astype(jnp.bfloat16).T

    by_width(width_ref, block, attend)


def bwd_kernel(
    width_ref, kv_ref, kvh_ref, kdoc_ref, qdoc_ref, qg_ref, out_ref, top_ref, inv_ref,
    dq_ref, dkv_lo_ref, dkv_hi_ref, dkvh_ref, k_s, v_s, kt_s, dk_s, dv_s,
):
    block = pl.program_id(0)

    @pl.when(block == 0)
    def _():
        for b, rows, k, v in key_blocks(kv_ref, kvh_ref):
            k_s[rows] = k
            v_s[rows] = v
            kt_s[b] = k.T
        dk_s[...] = jnp.zeros_like(dk_s)
        dv_s[...] = jnp.zeros_like(dv_s)

    def attend(width):
        first, rows = window_of(block, width)
        q = qg_ref[0, :TOK]
        grad = qg_ref[0, TOK:]
        grad_t = grad.T
        kt = jnp.concatenate([kt_s[first + n] for n in range(width)], 1)
        scores = masked_scores(k_s[rows], q, kdoc_ref[rows], qdoc_ref[0], width)
        weights = jnp.exp((scores - top_ref[0]) * SCALE) * inv_ref[0]
        probs = weights.astype(jnp.bfloat16)
        row_dot = jnp.sum(
            out_ref[0].T.astype(jnp.float32) * grad_t.astype(jnp.float32), 0, keepdims=True
        )
        prob_grad = dot_nn(v_s[rows], grad_t)
        score_grad = (weights * (prob_grad - row_dot)).astype(jnp.bfloat16)
        dq_ref[0] = (dot_nn(kt, score_grad) * SCALE).astype(jnp.bfloat16).T
        dk_s[rows] += dot_nn(score_grad, q)
        dv_s[rows] += dot_nn(probs, grad)

    by_width(width_ref, block, attend)

    @pl.when(block == ROW - 1)
    def _():
        outs = (dkvh_ref, dkv_lo_ref, dkv_hi_ref)
        for b in range(SPAN + ROW):
            rows = slice(b * TOK, (b + 1) * TOK)
            ref = outs[b // SPAN]
            ref[b % SPAN, :TOK] = (dk_s[rows] * SCALE).astype(ref.dtype)
            ref[b % SPAN, TOK:] = dv_s[rows].astype(ref.dtype)


KEYS = (SPAN + ROW) * TOK


def whole(*shape):
    return pl.BlockSpec(shape, lambda b, w: (0,) * len(shape))


def each(*shape):
    return pl.BlockSpec((1,) + shape, lambda b, w: (b, 0, 0))


SHARED_SPECS = [
    whole(ROW, 2 * TOK, HD),
    whole(SPAN, 2 * TOK, HD),
    whole(KEYS, HD),
    each(1, TOK),
    each(2 * TOK, HD),
]


def attention_fwd(widths, *operands):
    return pl.pallas_call(
        fwd_kernel,
        grid_spec=pltpu.PrefetchScalarGridSpec(
            num_scalar_prefetch=1,
            grid=(ROW,),
            in_specs=SHARED_SPECS,
            out_specs=[each(TOK, HD), each(1, TOK), each(1, TOK)],
            scratch_shapes=[
                pltpu.VMEM((KEYS, HD), jnp.bfloat16),
                pltpu.VMEM((SPAN + ROW, HD, TOK), jnp.bfloat16),
            ],
        ),
        out_shape=[
            jax.ShapeDtypeStruct((ROW, TOK, HD), jnp.bfloat16),
            jax.ShapeDtypeStruct((ROW, 1, TOK), jnp.float32),
            jax.ShapeDtypeStruct((ROW, 1, TOK), jnp.float32),
        ],
        compiler_params=pltpu.CompilerParams(vmem_limit_bytes=40 << 20),
        name="attn_fwd",
    )(widths, *operands)


def attention_bwd(widths, *operands):
    return pl.pallas_call(
        bwd_kernel,
        grid_spec=pltpu.PrefetchScalarGridSpec(
            num_scalar_prefetch=1,
            grid=(ROW,),
            in_specs=SHARED_SPECS + [each(TOK, HD), each(1, TOK), each(1, TOK)],
            out_specs=[each(TOK, HD)] + [whole(SPAN, 2 * TOK, HD)] * 3,
            scratch_shapes=[
                pltpu.VMEM((KEYS, HD), jnp.bfloat16),
                pltpu.VMEM((KEYS, HD), jnp.bfloat16),
                pltpu.VMEM((SPAN + ROW, HD, TOK), jnp.bfloat16),
                pltpu.VMEM((KEYS, HD), jnp.float32),
                pltpu.VMEM((KEYS, HD), jnp.float32),
            ],
        ),
        out_shape=[
            jax.ShapeDtypeStruct((ROW, TOK, HD), jnp.bfloat16),
            jax.ShapeDtypeStruct((SPAN, 2 * TOK, HD), jnp.bfloat16),
            jax.ShapeDtypeStruct((SPAN, 2 * TOK, HD), jnp.float32),
            jax.ShapeDtypeStruct((SPAN, 2 * TOK, HD), jnp.bfloat16),
        ],
        compiler_params=pltpu.CompilerParams(vmem_limit_bytes=40 << 20),
        name="attn_bwd",
    )(widths, *operands)


def per_device(
    queries_in, keys_in, values_in, gate_branch, key_branch, mr_filter, out_grad, doc_ids
):
    n_seq = lax.axis_size("seq")
    position = lax.axis_index("seq")
    rings = [list(range(g, g + ROW)) for g in range(0, n_seq, ROW)]

    def swap(x, groups=rings, axis="seq"):
        return lax.all_to_all(x, axis, 0, 0, axis_index_groups=groups, tiled=True)

    def shift(x, by):
        pairs = [(i, i + by) for i in range(n_seq) if 0 <= i + by < n_seq]
        return lax.ppermute(x, "seq", pairs)

    doc_front = jnp.concatenate([jnp.full((SPAN * TOK,), -1, jnp.int32), doc_ids], 0)
    docs = lax.dynamic_slice_in_dim(
        doc_front, (position // ROW) * (ROW * TOK), (SPAN + ROW) * TOK, 0
    ).reshape(SPAN + ROW, TOK)
    widths = jnp.ones((ROW,), jnp.int32)
    for back in range(1, SPAN + 1):
        widths = widths + (docs[SPAN - back : SPAN + ROW - back, -1] == docs[SPAN:, 0])
    kdoc = jnp.broadcast_to(docs.reshape(-1, 1), ((SPAN + ROW) * TOK, HD))
    qdoc = docs[SPAN:].reshape(ROW, 1, TOK)

    kv = swap(pack(keys_in, values_in))

    conv_grad = (out_grad.astype(jnp.float32) * gate_branch.astype(jnp.float32)).astype(
        jnp.bfloat16
    )
    grad_edge = shift(conv_grad[:TAPS], -1)
    mixed_grad = anti_conv(
        jnp.concatenate([conv_grad, grad_edge[: TAPS - 1]], 0), mr_filter
    )
    kvh = shift(kv[ROW - SPAN :], ROW)
    qg = swap(pack_grad(queries_in, mixed_grad, key_branch))

    shared = (widths, kv, kvh, kdoc, qdoc, qg)
    attn_head, top, inv = attention_fwd(*shared)
    attn_out = unpack(swap(attn_head))[0]
    dq_head, dkv_lo, dkv_hi, dkvh = attention_bwd(*shared, attn_head, top, inv)
    back = shift(dkvh, -ROW)
    dkv_hi = (dkv_hi + back.astype(jnp.float32)).astype(jnp.bfloat16)
    dqkv = jnp.concatenate([dq_head, jnp.concatenate([dkv_lo, dkv_hi], 0)], 1)
    query_grad, key_grad, value_grad = unpack(swap(dqkv))

    mixed = (key_branch.astype(jnp.float32) * attn_out.astype(jnp.float32)).astype(jnp.bfloat16)
    mixed_edge = shift(mixed[TOK - TAPS :], 1)
    mixed_ext = jnp.concatenate([mixed_edge[1:], mixed], 0)
    filter_part = anti_conv(mixed_ext, conv_grad)
    conv_out = causal_conv(mixed_ext, mr_filter)
    gate_grad = (out_grad.astype(jnp.float32) * conv_out).astype(jnp.bfloat16)
    branch_grad = (mixed_grad * attn_out.astype(jnp.float32)).astype(jnp.bfloat16)

    tap_rows = TAPS // n_seq
    parts = jnp.flip(filter_part, 0).astype(jnp.bfloat16)
    parts = swap(parts.reshape(n_seq, tap_rows, -1), None)
    own_grad = jnp.sum(parts.astype(jnp.float32), 0)
    own_filter = lax.dynamic_slice_in_dim(mr_filter, position * tap_rows, tap_rows, 0)
    norms = jnp.stack(
        [jnp.sum(jnp.square(own_filter.astype(jnp.float32))), jnp.sum(own_grad * own_grad)]
    )
    norms = jnp.broadcast_to(norms[:, None], (2, HD))
    hops = [("ch", 1), ("ch", 2), ("ch", 4)] + [("seq", h) for h in (8, 16, 1, 2, 4)]
    for axis, hop in hops:
        pairs = [(i, i ^ hop) for i in range(lax.axis_size(axis))]
        norms = norms + lax.ppermute(norms, axis, pairs)
    trust = jnp.sqrt(norms[0, 0]) / jnp.sqrt(norms[1, 0] + 1e-06)
    filter_step = trust * own_grad
    return (query_grad, key_grad, value_grad, gate_grad, branch_grad, filter_step)


def solution(mesh):
    rows = P("seq", "ch")
    return jax.shard_map(
        per_device,
        mesh=mesh,
        in_specs=(rows, rows, rows, rows, rows, P(None, "ch"), rows, P()),
        out_specs=(rows,) * 6,
        check_vma=False,
    )
```

```python
import jax
import jax.numpy as jnp
from jax import lax
from jax.experimental import pallas as pl
from jax.experimental.pallas import tpu as pltpu
from jax.sharding import PartitionSpec as P


HD = 128
TAPS = 128
SPAN = 4
ROW = 8
TOK = 256
EXT = TOK + TAPS
NEG = -1e30
STEP = 4
SCALE = HD ** (-0.5)


def causal_conv(extended, weights_in):
    kernel = jnp.flip(weights_in, 0)[:, None, :]
    return lax.conv_general_dilated(
        extended[None],
        kernel,
        (1,),
        "VALID",
        dimension_numbers=("NWC", "WIO", "NWC"),
        feature_group_count=extended.shape[1],
        preferred_element_type=jnp.float32,
    )[0]


def anti_conv(extended, weights_in):
    return lax.conv_general_dilated(
        extended[None],
        weights_in[:, None, :],
        (1,),
        "VALID",
        dimension_numbers=("NWC", "WIO", "NWC"),
        feature_group_count=extended.shape[1],
        preferred_element_type=jnp.float32,
    )[0]


def pack_kernel(*refs):
    *in_refs, out_ref = refs
    for head in range(out_ref.shape[0]):
        for n, in_ref in enumerate(in_refs):
            out_ref[head, n * TOK : (n + 1) * TOK] = in_ref[:, head * HD : (head + 1) * HD]


def pack(*arrays):
    heads = arrays[0].shape[1] // HD
    n = len(arrays)
    return pl.pallas_call(
        pack_kernel,
        grid=(heads // STEP,),
        in_specs=[pl.BlockSpec((TOK, STEP * HD), lambda h: (0, h))] * n,
        out_specs=pl.BlockSpec((STEP, n * TOK, HD), lambda h: (h, 0, 0)),
        out_shape=jax.ShapeDtypeStruct((heads, n * TOK, HD), arrays[0].dtype),
        name="pack",
    )(*arrays)


def unpack_kernel(x_ref, *out_refs):
    for head in range(x_ref.shape[0]):
        for n, out_ref in enumerate(out_refs):
            out_ref[:, head * HD : (head + 1) * HD] = x_ref[head, n * TOK : (n + 1) * TOK]


def unpack(x):
    heads, rows, _ = x.shape
    n = rows // TOK
    return pl.pallas_call(
        unpack_kernel,
        grid=(heads // STEP,),
        in_specs=[pl.BlockSpec((STEP, rows, HD), lambda h: (h, 0, 0))],
        out_specs=[pl.BlockSpec((TOK, STEP * HD), lambda h: (0, h))] * n,
        out_shape=[jax.ShapeDtypeStruct((TOK, heads * HD), x.dtype)] * n,
        name="unpack",
    )(x)


def spread(tile_refs, ext_s, sh_s):
    at = 0
    for piece in tile_refs:
        ext_s[at : at + piece.shape[0]] = piece.astype(jnp.float32)
        at += piece.shape[0]
    ext_s[at:] = jnp.zeros((8, HD), jnp.float32)
    for r in range(8):
        sh_s[r] = ext_s[pl.ds(r, EXT)]


def head_anti_kernel(cur_ref, next_ref, edge_ref, w_ref, out_ref, ext_s, sh_s, w_s):
    last = pl.program_id(0) == ROW - 1
    after = jnp.where(last, edge_ref[...].astype(jnp.float32), next_ref[0].astype(jnp.float32))
    spread((cur_ref[0], after), ext_s, sh_s)
    w_s[...] = w_ref[...].astype(jnp.float32)
    rows = TOK // 2
    for half in range(2):

        def group(k, total, half=half):
            taps = w_s[pl.ds(pl.multiple_of(k * 8, 8), 8)]
            start = pl.multiple_of(k * 8 + half * rows, 8)
            for r in range(8):
                total = total + taps[r : r + 1] * sh_s[r, pl.ds(start, rows)]
            return total

        out_ref[0, half * rows : (half + 1) * rows] = lax.fori_loop(
            0, TAPS // 8, group, jnp.zeros((rows, HD), jnp.float32)
        )


def head_anti(packed, edge, weights):
    return pl.pallas_call(
        head_anti_kernel,
        grid=(ROW,),
        in_specs=[
            pl.BlockSpec((1, TOK, HD), lambda b: (b, 0, 0)),
            pl.BlockSpec((1, TAPS, HD), lambda b: (jnp.minimum(b + 1, ROW - 1), 0, 0)),
            pl.BlockSpec((TAPS, HD), lambda b: (0, 0)),
            pl.BlockSpec((TAPS, HD), lambda b: (0, 0)),
        ],
        out_specs=pl.BlockSpec((1, TOK, HD), lambda b: (b, 0, 0)),
        out_shape=jax.ShapeDtypeStruct((ROW, TOK, HD), jnp.float32),
        scratch_shapes=[
            pltpu.VMEM((EXT + 8, HD), jnp.float32),
            pltpu.VMEM((8, EXT, HD), jnp.float32),
            pltpu.VMEM((TAPS, HD), jnp.float32),
        ],
        name="head_anti",
    )(packed, packed, edge, weights)


def head_corr_kernel(cur_ref, prev_ref, edge_ref, g_ref, out_ref, ext_s, sh_s, g_s, part_s):
    block = pl.program_id(0)
    before = jnp.where(
        block == 0, edge_ref[...].astype(jnp.float32), prev_ref[0].astype(jnp.float32)
    )
    spread((before, cur_ref[0]), ext_s, sh_s)
    g_s[...] = g_ref[0].astype(jnp.float32)

    @pl.when(block == 0)
    def _():
        part_s[...] = jnp.zeros_like(part_s)

    rows = TOK // 2

    def half_of(half, _):
        base = pl.multiple_of(half * rows, rows)
        g = [g_s[pl.ds(base + 8 * i, 8)] for i in range(rows // 8)]
        for r in range(8):
            for group in range(2):
                low = (72 if r == 0 else 64) - 64 * group
                piece = [
                    sh_s[(8 - r) % 8, pl.ds(base + low + 8 * i, 8)] for i in range(rows // 8 + 7)
                ]
                for kk in range(8):
                    total = g[0] * piece[7 - kk]
                    for i in range(1, rows // 8):
                        total = total + g[i] * piece[i + 7 - kk]
                    part_s[r, 8 * group + kk] += total
        return 0

    lax.fori_loop(0, 2, half_of, 0)

    @pl.when(block == ROW - 1)
    def _():
        for r in range(8):
            out_ref[pl.ds(r, TAPS // 8, stride=8)] = jnp.sum(part_s[r], 1)


def head_corr(mixed, edge, packed):
    return pl.pallas_call(
        head_corr_kernel,
        grid=(ROW,),
        in_specs=[
            pl.BlockSpec((1, TOK, HD), lambda b: (b, 0, 0)),
            pl.BlockSpec((1, TAPS, HD), lambda b: (jnp.maximum(b - 1, 0), 1, 0)),
            pl.BlockSpec((TAPS, HD), lambda b: (0, 0)),
            pl.BlockSpec((1, TOK, HD), lambda b: (b, 0, 0)),
        ],
        out_specs=pl.BlockSpec((TAPS, HD), lambda b: (0, 0)),
        out_shape=jax.ShapeDtypeStruct((TAPS, HD), jnp.float32),
        scratch_shapes=[
            pltpu.VMEM((EXT + 8, HD), jnp.float32),
            pltpu.VMEM((8, EXT, HD), jnp.float32),
            pltpu.VMEM((TOK, HD), jnp.float32),
            pltpu.VMEM((8, TAPS // 8, 8, HD), jnp.float32),
        ],
        name="head_corr",
    )(mixed, mixed, edge, packed)


def dot_nn(a, b):
    return jnp.dot(a, b, preferred_element_type=jnp.float32)


def window_of(block, width):
    first = block + (SPAN + 1 - width)
    return first, pl.ds(pl.multiple_of(first * TOK, TOK), width * TOK)


def key_blocks(packed_ref, kvh_ref):
    for b in range(SPAN + ROW):
        src = kvh_ref if b < SPAN else packed_ref
        at = b if b < SPAN else b - SPAN
        skip = 0 if b < SPAN else TOK
        k = src[at, skip : skip + TOK]
        yield b, slice(b * TOK, (b + 1) * TOK), k, src[at, skip + TOK :]


def masked_scores(k, q, kdoc, qdoc, width):
    scores = dot_nn(k, q.T)
    same = jnp.concatenate([kdoc, kdoc], 1) == qdoc
    key_at = lax.broadcasted_iota(jnp.int32, scores.shape, 0)
    query_at = lax.broadcasted_iota(jnp.int32, scores.shape, 1) + (width - 1) * TOK
    return jnp.where(same & (key_at <= query_at), scores, NEG)


def by_width(width_ref, block, attend):
    for width in range(1, SPAN + 2):
        pl.when(width_ref[block] == width)(lambda width=width: attend(width))


def fwd_kernel(
    width_ref, packed_ref, kvh_ref, kdoc_ref, qdoc_ref, qk_ref,
    out_ref, mixed_ref, top_ref, inv_ref, k_s, vt_s,
):
    block = pl.program_id(0)

    @pl.when(block == 0)
    def _():
        for b, rows, k, v in key_blocks(packed_ref, kvh_ref):
            k_s[rows] = k
            vt_s[b] = v.T

    def attend(width):
        first, rows = window_of(block, width)
        q = qk_ref[0, :TOK]
        vt = jnp.concatenate([vt_s[first + n] for n in range(width)], 1)
        scores = masked_scores(k_s[rows], q, kdoc_ref[rows], qdoc_ref[0], width)
        top = jnp.max(scores, 0, keepdims=True)
        weights = jnp.exp((scores - top) * SCALE)
        inv = 1.0 / jnp.sum(weights, 0, keepdims=True)
        top_ref[0] = top
        inv_ref[0] = inv
        probs = (weights * inv).astype(jnp.bfloat16)
        out = dot_nn(vt, probs).astype(jnp.bfloat16).T
        out_ref[0] = out
        key = qk_ref[0, TOK:].astype(jnp.float32)
        mixed_ref[0] = (key * out.astype(jnp.float32)).astype(jnp.bfloat16)

    by_width(width_ref, block, attend)


def bwd_kernel(
    width_ref, packed_ref, kvh_ref, kdoc_ref, qdoc_ref, qk_ref, mixed_grad_ref,
    out_ref, top_ref, inv_ref,
    dq_ref, dkv_lo_ref, dkv_hi_ref, dkvh_ref, k_s, v_s, kt_s, dk_s, dv_s,
):
    block = pl.program_id(0)

    @pl.when(block == 0)
    def _():
        for b, rows, k, v in key_blocks(packed_ref, kvh_ref):
            k_s[rows] = k
            v_s[rows] = v
            kt_s[b] = k.T
        dk_s[...] = jnp.zeros_like(dk_s)
        dv_s[...] = jnp.zeros_like(dv_s)

    def attend(width):
        first, rows = window_of(block, width)
        q = qk_ref[0, :TOK]
        key = qk_ref[0, TOK:].astype(jnp.float32)
        grad = (mixed_grad_ref[0] * key).astype(jnp.bfloat16)
        grad_t = grad.T
        kt = jnp.concatenate([kt_s[first + n] for n in range(width)], 1)
        scores = masked_scores(k_s[rows], q, kdoc_ref[rows], qdoc_ref[0], width)
        weights = jnp.exp((scores - top_ref[0]) * SCALE) * inv_ref[0]
        probs = weights.astype(jnp.bfloat16)
        row_dot = jnp.sum(
            out_ref[0].T.astype(jnp.float32) * grad_t.astype(jnp.float32), 0, keepdims=True
        )
        prob_grad = dot_nn(v_s[rows], grad_t)
        score_grad = (weights * (prob_grad - row_dot)).astype(jnp.bfloat16)
        dq_ref[0] = (dot_nn(kt, score_grad) * SCALE).astype(jnp.bfloat16).T
        dk_s[rows] += dot_nn(score_grad, q)
        dv_s[rows] += dot_nn(probs, grad)

    by_width(width_ref, block, attend)

    @pl.when(block == ROW - 1)
    def _():
        outs = (dkvh_ref, dkv_lo_ref, dkv_hi_ref)
        for b in range(SPAN + ROW):
            rows = slice(b * TOK, (b + 1) * TOK)
            ref = outs[b // SPAN]
            ref[b % SPAN, :TOK] = (dk_s[rows] * SCALE).astype(ref.dtype)
            ref[b % SPAN, TOK:] = dv_s[rows].astype(ref.dtype)


KEYS = (SPAN + ROW) * TOK


def whole(*shape):
    return pl.BlockSpec(shape, lambda b, w: (0,) * len(shape))


def each(*shape):
    return pl.BlockSpec((1,) + shape, lambda b, w: (b, 0, 0))


SHARED_SPECS = [
    whole(ROW, 3 * TOK, HD),
    whole(SPAN, 2 * TOK, HD),
    whole(KEYS, HD),
    each(1, TOK),
    each(2 * TOK, HD),
]


def attention_fwd(widths, *operands):
    return pl.pallas_call(
        fwd_kernel,
        grid_spec=pltpu.PrefetchScalarGridSpec(
            num_scalar_prefetch=1,
            grid=(ROW,),
            in_specs=SHARED_SPECS,
            out_specs=[each(TOK, HD), each(TOK, HD), each(1, TOK), each(1, TOK)],
            scratch_shapes=[
                pltpu.VMEM((KEYS, HD), jnp.bfloat16),
                pltpu.VMEM((SPAN + ROW, HD, TOK), jnp.bfloat16),
            ],
        ),
        out_shape=[
            jax.ShapeDtypeStruct((ROW, TOK, HD), jnp.bfloat16),
            jax.ShapeDtypeStruct((ROW, TOK, HD), jnp.bfloat16),
            jax.ShapeDtypeStruct((ROW, 1, TOK), jnp.float32),
            jax.ShapeDtypeStruct((ROW, 1, TOK), jnp.float32),
        ],
        compiler_params=pltpu.CompilerParams(vmem_limit_bytes=40 << 20),
        name="attn_fwd",
    )(widths, *operands)


def attention_bwd(widths, *operands):
    return pl.pallas_call(
        bwd_kernel,
        grid_spec=pltpu.PrefetchScalarGridSpec(
            num_scalar_prefetch=1,
            grid=(ROW,),
            in_specs=SHARED_SPECS + [each(TOK, HD), each(TOK, HD), each(1, TOK), each(1, TOK)],
            out_specs=[each(TOK, HD)] + [whole(SPAN, 2 * TOK, HD)] * 3,
            scratch_shapes=[
                pltpu.VMEM((KEYS, HD), jnp.bfloat16),
                pltpu.VMEM((KEYS, HD), jnp.bfloat16),
                pltpu.VMEM((SPAN + ROW, HD, TOK), jnp.bfloat16),
                pltpu.VMEM((KEYS, HD), jnp.float32),
                pltpu.VMEM((KEYS, HD), jnp.float32),
            ],
        ),
        out_shape=[
            jax.ShapeDtypeStruct((ROW, TOK, HD), jnp.bfloat16),
            jax.ShapeDtypeStruct((SPAN, 2 * TOK, HD), jnp.bfloat16),
            jax.ShapeDtypeStruct((SPAN, 2 * TOK, HD), jnp.float32),
            jax.ShapeDtypeStruct((SPAN, 2 * TOK, HD), jnp.bfloat16),
        ],
        compiler_params=pltpu.CompilerParams(vmem_limit_bytes=40 << 20),
        name="attn_bwd",
    )(widths, *operands)


def per_device(
    queries_in, keys_in, values_in, gate_branch, key_branch, mr_filter, out_grad, doc_ids
):
    n_seq = lax.axis_size("seq")
    position = lax.axis_index("seq")
    rings = [list(range(g, g + ROW)) for g in range(0, n_seq, ROW)]

    def swap(x, groups=rings, axis="seq"):
        return lax.all_to_all(x, axis, 0, 0, axis_index_groups=groups, tiled=True)

    def shift(x, by):
        pairs = [(i, i + by) for i in range(n_seq) if 0 <= i + by < n_seq]
        return lax.ppermute(x, "seq", pairs)

    doc_front = jnp.concatenate([jnp.full((SPAN * TOK,), -1, jnp.int32), doc_ids], 0)
    docs = lax.dynamic_slice_in_dim(
        doc_front, (position // ROW) * (ROW * TOK), (SPAN + ROW) * TOK, 0
    ).reshape(SPAN + ROW, TOK)
    widths = jnp.ones((ROW,), jnp.int32)
    for back in range(1, SPAN + 1):
        widths = widths + (docs[SPAN - back : SPAN + ROW - back, -1] == docs[SPAN:, 0])
    kdoc = jnp.broadcast_to(docs.reshape(-1, 1), ((SPAN + ROW) * TOK, HD))
    qdoc = docs[SPAN:].reshape(ROW, 1, TOK)

    conv_grad = (out_grad.astype(jnp.float32) * gate_branch.astype(jnp.float32)).astype(
        jnp.bfloat16
    )
    grad_edge = shift(conv_grad[:TAPS], -1)
    packed = swap(pack(conv_grad, keys_in, values_in))
    mixed_grad = anti_conv(
        jnp.concatenate([conv_grad, grad_edge[: TAPS - 1]], 0), mr_filter
    )
    qk = swap(pack(queries_in, key_branch))

    kvh = shift(packed[ROW - SPAN :, TOK:], ROW)
    head_edge = shift(packed[0, :TAPS], -ROW)
    head = position % ROW
    own_taps = lax.dynamic_slice_in_dim(mr_filter, head * HD, HD, 1)
    mixed_grad_head = head_anti(packed, head_edge, own_taps)

    shared = (widths, packed, kvh, kdoc, qdoc, qk)
    attn_head, mixed_head, top, inv = attention_fwd(*shared)
    attn_out = unpack(swap(attn_head))[0]
    mixed_before = shift(mixed_head[ROW - 1, TOK - TAPS :], ROW)
    dq_head, dkv_lo, dkv_hi, dkvh = attention_bwd(
        *shared, mixed_grad_head, attn_head, top, inv
    )
    back = shift(dkvh, -ROW)
    filter_part = head_corr(mixed_head, mixed_before, packed)
    dkv_hi = (dkv_hi + back.astype(jnp.float32)).astype(jnp.bfloat16)
    dqkv = jnp.concatenate([dq_head, jnp.concatenate([dkv_lo, dkv_hi], 0)], 1)
    query_grad, key_grad, value_grad = unpack(swap(dqkv))

    mixed = (key_branch.astype(jnp.float32) * attn_out.astype(jnp.float32)).astype(jnp.bfloat16)
    mixed_edge = shift(mixed[TOK - TAPS :], 1)
    mixed_ext = jnp.concatenate([mixed_edge[1:], mixed], 0)
    conv_out = causal_conv(mixed_ext, mr_filter)
    gate_grad = (out_grad.astype(jnp.float32) * conv_out).astype(jnp.bfloat16)
    branch_grad = (mixed_grad * attn_out.astype(jnp.float32)).astype(jnp.bfloat16)

    def meet(x, axis, hop):
        pairs = [(i, i ^ hop) for i in range(lax.axis_size(axis))]
        return x + lax.ppermute(x, axis, pairs)

    rings_n = n_seq // ROW
    filter_grad = filter_part
    hop = ROW
    while hop < n_seq:
        filter_grad = meet(filter_grad, "seq", hop)
        hop *= 2
    tap_share = TAPS // ROW
    own_filter = lax.dynamic_slice_in_dim(mr_filter, head * tap_share, tap_share, 0)
    norms = jnp.stack(
        [jnp.sum(jnp.square(own_filter.astype(jnp.float32))), jnp.sum(filter_grad * filter_grad)]
    )
    norms = jnp.broadcast_to(norms[:, None], (2, HD))
    hop = 1
    while hop < lax.axis_size("ch"):
        norms = meet(norms, "ch", hop)
        hop *= 2
    tap_rows = TAPS // n_seq
    ring_taps = lax.dynamic_slice_in_dim(
        filter_grad, (position // ROW) * (TAPS // rings_n), TAPS // rings_n, 0
    ).reshape(ROW, tap_rows, HD)
    sent = jnp.concatenate([ring_taps, jnp.broadcast_to(norms[None], (ROW, 2, HD))], 1)
    got = swap(sent)
    own_grad = jnp.swapaxes(got[:, :tap_rows], 0, 1).reshape(tap_rows, ROW * HD)
    norms = jnp.sum(got[:, tap_rows:], 0)
    trust = jnp.sqrt(norms[0, 0]) / jnp.sqrt(norms[1, 0] + 1e-06)
    filter_step = trust * own_grad
    return (query_grad, key_grad, value_grad, gate_grad, branch_grad, filter_step)


def solution(mesh):
    rows = P("seq", "ch")
    return jax.shard_map(
        per_device,
        mesh=mesh,
        in_specs=(rows, rows, rows, rows, rows, P(None, "ch"), rows, P()),
        out_specs=(rows,) * 6,
        check_vma=False,
    )
```

```python
import jax
import jax.numpy as jnp
from jax import lax
from jax.experimental import pallas as pl
from jax.experimental.pallas import tpu as pltpu
from jax.sharding import PartitionSpec as P


HD = 128
TAPS = 128
SPAN = 4
ROW = 8
TOK = 256
EXT = TOK + TAPS
NEG = -1e30
STEP = 4
SCALE = HD ** (-0.5)
PIECES = 4


def anti_conv(extended, weights_in):
    return lax.conv_general_dilated(
        extended[None],
        weights_in[:, None, :],
        (1,),
        "VALID",
        dimension_numbers=("NWC", "WIO", "NWC"),
        feature_group_count=extended.shape[1],
        preferred_element_type=jnp.float32,
    )[0]


def hbm(*arrays):
    return [pltpu.with_memory_space_constraint(x, pltpu.HBM) for x in arrays]


def pack_kernel(*refs):
    *in_refs, out_ref = refs
    for head in range(out_ref.shape[0]):
        for n, in_ref in enumerate(in_refs):
            out_ref[head, n * TOK : (n + 1) * TOK] = in_ref[:, head * HD : (head + 1) * HD]


def pack(*arrays):
    heads = arrays[0].shape[1] // HD
    n = len(arrays)
    return pl.pallas_call(
        pack_kernel,
        grid=(heads // STEP,),
        in_specs=[pl.BlockSpec((TOK, STEP * HD), lambda h: (0, h))] * n,
        out_specs=pl.BlockSpec((STEP, n * TOK, HD), lambda h: (h, 0, 0)),
        out_shape=pltpu.HBM((heads, n * TOK, HD), arrays[0].dtype),
        name="pack",
    )(*arrays)


def unpack_kernel(x_ref, *out_refs):
    for head in range(x_ref.shape[0]):
        for n, out_ref in enumerate(out_refs):
            out_ref[:, head * HD : (head + 1) * HD] = x_ref[head, n * TOK : (n + 1) * TOK]


def unpack(x):
    heads, rows, _ = x.shape
    n = rows // TOK
    return pl.pallas_call(
        unpack_kernel,
        grid=(heads // STEP,),
        in_specs=[pl.BlockSpec((STEP, rows, HD), lambda h: (h, 0, 0))],
        out_specs=[pl.BlockSpec((TOK, STEP * HD), lambda h: (0, h))] * n,
        out_shape=[jax.ShapeDtypeStruct((TOK, heads * HD), x.dtype)] * n,
        name="unpack",
    )(*hbm(x))


def finish_kernel(x_ref, key_ref, mixed_grad_ref, mixed_ref, branch_ref):
    for head in range(x_ref.shape[0]):
        lanes = slice(head * HD, (head + 1) * HD)
        attn_out = x_ref[head].astype(jnp.float32)
        mixed_ref[:, lanes] = (key_ref[:, lanes].astype(jnp.float32) * attn_out).astype(
            jnp.bfloat16
        )
        branch_ref[:, lanes] = (mixed_grad_ref[:, lanes] * attn_out).astype(jnp.bfloat16)


def finish(attn_out, key, mixed_grad):
    heads = attn_out.shape[0]
    column = pl.BlockSpec((TOK, STEP * HD), lambda h: (0, h))
    shape = jax.ShapeDtypeStruct((TOK, heads * HD), jnp.bfloat16)
    return pl.pallas_call(
        finish_kernel,
        grid=(heads // STEP,),
        in_specs=[pl.BlockSpec((STEP, TOK, HD), lambda h: (h, 0, 0)), column, column],
        out_specs=[column] * 2,
        out_shape=[shape] * 2,
        name="finish",
    )(*hbm(attn_out), key, mixed_grad)


def join_kernel(joined_ref, own_ref, back_ref, out_ref):
    out_ref[...] = (own_ref[...] + back_ref[...].astype(jnp.float32)).astype(jnp.bfloat16)


def join(joined, own, back):
    part = pl.BlockSpec((2, 2 * TOK, HD), lambda b: (b, 0, 0))
    first = (ROW - SPAN) // 2
    return pl.pallas_call(
        join_kernel,
        grid=(SPAN // 2,),
        in_specs=[pl.BlockSpec(memory_space=pl.ANY), part, part],
        out_specs=pl.BlockSpec((2, 2 * TOK, HD), lambda b: (b + first, 0, 0)),
        out_shape=pltpu.HBM(joined.shape, joined.dtype),
        input_output_aliases={0: 0},
        name="join",
    )(*hbm(joined, own, back))


def spread(tile_refs, ext_s, sh_s):
    at = 0
    for piece in tile_refs:
        ext_s[at : at + piece.shape[0]] = piece.astype(jnp.float32)
        at += piece.shape[0]
    ext_s[at:] = jnp.zeros((8, HD), jnp.float32)
    for r in range(8):
        sh_s[r] = ext_s[pl.ds(r, EXT)]


HALF = TOK // 2


def ahead(k, r):
    return r, k * 8


def behind(k, r):
    return ((8 - r) % 8, TAPS - 8 - k * 8) if r else (0, TAPS - k * 8)


def filtered(sh_s, w_s, where, half):
    def group(k, total):
        taps = w_s[pl.ds(pl.multiple_of(k * 8, 8), 8)]
        for r in range(8):
            slot, start = where(k, r)
            start = pl.multiple_of(start + half * HALF, 8)
            total = total + taps[r : r + 1] * sh_s[slot, pl.ds(start, HALF)]
        return total

    return lax.fori_loop(0, TAPS // 8, group, jnp.zeros((HALF, HD), jnp.float32))


def causal_kernel(m_ref, edge_ref, w_ref, grad_ref, *refs):
    out_ref, ext_s, sh_s, w_s = refs[-4:]
    spread((edge_ref[...], m_ref[...]), ext_s, sh_s)
    w_s[...] = w_ref[...].astype(jnp.float32)
    for half in range(2):
        rows = slice(half * HALF, (half + 1) * HALF)
        conv_out = filtered(sh_s, w_s, behind, half)
        out_ref[rows] = (grad_ref[rows].astype(jnp.float32) * conv_out).astype(jnp.bfloat16)


def causal_piece(piece, mixed, edge, weights, out_grad, before):
    tiles = mixed.shape[1] // HD // PIECES
    column = lambda rows: pl.BlockSpec((rows, HD), lambda c: (0, c + piece * tiles))
    return pl.pallas_call(
        causal_kernel,
        grid=(tiles,),
        in_specs=[column(TOK), column(TAPS), column(TAPS), column(TOK)]
        + [pl.BlockSpec(memory_space=pl.ANY)] * len(before),
        out_specs=column(TOK),
        out_shape=pltpu.HBM(mixed.shape, jnp.bfloat16),
        scratch_shapes=[
            pltpu.VMEM((EXT + 8, HD), jnp.float32),
            pltpu.VMEM((8, EXT, HD), jnp.float32),
            pltpu.VMEM((TAPS, HD), jnp.float32),
        ],
        input_output_aliases={4: 0} if before else {},
        name="causal",
    )(mixed, edge, weights, out_grad, *hbm(*before))


def head_anti_kernel(cur_ref, next_ref, edge_ref, w_ref, out_ref, ext_s, sh_s, w_s):
    last = pl.program_id(0) == ROW - 1
    after = jnp.where(last, edge_ref[...].astype(jnp.float32), next_ref[0].astype(jnp.float32))
    spread((cur_ref[0], after), ext_s, sh_s)
    w_s[...] = w_ref[...].astype(jnp.float32)
    for half in range(2):
        out_ref[0, half * HALF : (half + 1) * HALF] = filtered(sh_s, w_s, ahead, half)


def head_anti(packed, edge, weights):
    return pl.pallas_call(
        head_anti_kernel,
        grid=(ROW,),
        in_specs=[
            pl.BlockSpec((1, TOK, HD), lambda b: (b, 0, 0)),
            pl.BlockSpec((1, TAPS, HD), lambda b: (jnp.minimum(b + 1, ROW - 1), 0, 0)),
            pl.BlockSpec((TAPS, HD), lambda b: (0, 0)),
            pl.BlockSpec((TAPS, HD), lambda b: (0, 0)),
        ],
        out_specs=pl.BlockSpec((1, TOK, HD), lambda b: (b, 0, 0)),
        out_shape=pltpu.HBM((ROW, TOK, HD), jnp.float32),
        scratch_shapes=[
            pltpu.VMEM((EXT + 8, HD), jnp.float32),
            pltpu.VMEM((8, EXT, HD), jnp.float32),
            pltpu.VMEM((TAPS, HD), jnp.float32),
        ],
        name="head_anti",
    )(*hbm(packed, packed), edge, weights)


def head_corr_kernel(cur_ref, prev_ref, edge_ref, g_ref, out_ref, ext_s, sh_s, g_s, part_s):
    block = pl.program_id(0)
    before = jnp.where(
        block == 0, edge_ref[...].astype(jnp.float32), prev_ref[0].astype(jnp.float32)
    )
    spread((before, cur_ref[0]), ext_s, sh_s)
    g_s[...] = g_ref[0].astype(jnp.float32)

    @pl.when(block == 0)
    def _():
        part_s[...] = jnp.zeros_like(part_s)

    rows = TOK // 2

    def half_of(half, _):
        base = pl.multiple_of(half * rows, rows)
        g = [g_s[pl.ds(base + 8 * i, 8)] for i in range(rows // 8)]
        for r in range(8):
            for group in range(2):
                low = (72 if r == 0 else 64) - 64 * group
                piece = [
                    sh_s[(8 - r) % 8, pl.ds(base + low + 8 * i, 8)] for i in range(rows // 8 + 7)
                ]
                for kk in range(8):
                    total = g[0] * piece[7 - kk]
                    for i in range(1, rows // 8):
                        total = total + g[i] * piece[i + 7 - kk]
                    part_s[r, 8 * group + kk] += total
        return 0

    lax.fori_loop(0, 2, half_of, 0)

    @pl.when(block == ROW - 1)
    def _():
        for r in range(8):
            out_ref[pl.ds(r, TAPS // 8, stride=8)] = jnp.sum(part_s[r], 1)


def head_corr(mixed, edge, packed):
    return pl.pallas_call(
        head_corr_kernel,
        grid=(ROW,),
        in_specs=[
            pl.BlockSpec((1, TOK, HD), lambda b: (b, 0, 0)),
            pl.BlockSpec((1, TAPS, HD), lambda b: (jnp.maximum(b - 1, 0), 1, 0)),
            pl.BlockSpec((TAPS, HD), lambda b: (0, 0)),
            pl.BlockSpec((1, TOK, HD), lambda b: (b, 0, 0)),
        ],
        out_specs=pl.BlockSpec((TAPS, HD), lambda b: (0, 0)),
        out_shape=jax.ShapeDtypeStruct((TAPS, HD), jnp.float32),
        scratch_shapes=[
            pltpu.VMEM((EXT + 8, HD), jnp.float32),
            pltpu.VMEM((8, EXT, HD), jnp.float32),
            pltpu.VMEM((TOK, HD), jnp.float32),
            pltpu.VMEM((8, TAPS // 8, 8, HD), jnp.float32),
        ],
        name="head_corr",
    )(*hbm(mixed, mixed), edge, *hbm(packed))


def dot_nn(a, b):
    return jnp.dot(a, b, preferred_element_type=jnp.float32)


def window_of(block, width):
    first = block + (SPAN + 1 - width)
    return first, pl.ds(pl.multiple_of(first * TOK, TOK), width * TOK)


def key_blocks(packed_ref, kvh_ref):
    for b in range(SPAN + ROW):
        src = kvh_ref if b < SPAN else packed_ref
        at = b if b < SPAN else b - SPAN
        skip = 0 if b < SPAN else TOK
        k = src[at, skip : skip + TOK]
        yield b, slice(b * TOK, (b + 1) * TOK), k, src[at, skip + TOK :]


def masked_scores(k, q, kdoc, qdoc, width):
    scores = dot_nn(k, q.T)
    same = jnp.concatenate([kdoc, kdoc], 1) == qdoc
    key_at = lax.broadcasted_iota(jnp.int32, scores.shape, 0)
    query_at = lax.broadcasted_iota(jnp.int32, scores.shape, 1) + (width - 1) * TOK
    return jnp.where(same & (key_at <= query_at), scores, NEG)


def by_width(width_ref, block, attend):
    for width in range(1, SPAN + 2):
        pl.when(width_ref[block] == width)(lambda width=width: attend(width))


def fwd_kernel(
    width_ref, packed_ref, kvh_ref, kdoc_ref, qdoc_ref, qk_ref,
    out_ref, mixed_ref, top_ref, inv_ref, k_s, vt_s,
):
    block = pl.program_id(0)

    @pl.when(block == 0)
    def _():
        for b, rows, k, v in key_blocks(packed_ref, kvh_ref):
            k_s[rows] = k
            vt_s[b] = v.T

    def attend(width):
        first, rows = window_of(block, width)
        q = qk_ref[0, :TOK]
        vt = jnp.concatenate([vt_s[first + n] for n in range(width)], 1)
        scores = masked_scores(k_s[rows], q, kdoc_ref[rows], qdoc_ref[0], width)
        top = jnp.max(scores, 0, keepdims=True)
        weights = jnp.exp((scores - top) * SCALE)
        inv = 1.0 / jnp.sum(weights, 0, keepdims=True)
        top_ref[0] = top
        inv_ref[0] = inv
        probs = (weights * inv).astype(jnp.bfloat16)
        out = dot_nn(vt, probs).astype(jnp.bfloat16).T
        out_ref[0] = out
        key = qk_ref[0, TOK:].astype(jnp.float32)
        mixed_ref[0] = (key * out.astype(jnp.float32)).astype(jnp.bfloat16)

    by_width(width_ref, block, attend)


def bwd_kernel(
    width_ref, packed_ref, kvh_ref, kdoc_ref, qdoc_ref, qk_ref, mixed_grad_ref,
    out_ref, top_ref, inv_ref,
    joined_ref, dkv_hi_ref, dkvh_ref, k_s, v_s, kt_s, dk_s, dv_s,
):
    block = pl.program_id(0)

    @pl.when(block == 0)
    def _():
        for b, rows, k, v in key_blocks(packed_ref, kvh_ref):
            k_s[rows] = k
            v_s[rows] = v
            kt_s[b] = k.T
        dk_s[...] = jnp.zeros_like(dk_s)
        dv_s[...] = jnp.zeros_like(dv_s)

    def attend(width):
        first, rows = window_of(block, width)
        q = qk_ref[0, :TOK]
        key = qk_ref[0, TOK:].astype(jnp.float32)
        grad = (mixed_grad_ref[0] * key).astype(jnp.bfloat16)
        grad_t = grad.T
        kt = jnp.concatenate([kt_s[first + n] for n in range(width)], 1)
        scores = masked_scores(k_s[rows], q, kdoc_ref[rows], qdoc_ref[0], width)
        weights = jnp.exp((scores - top_ref[0]) * SCALE) * inv_ref[0]
        probs = weights.astype(jnp.bfloat16)
        row_dot = jnp.sum(
            out_ref[0].T.astype(jnp.float32) * grad_t.astype(jnp.float32), 0, keepdims=True
        )
        prob_grad = dot_nn(v_s[rows], grad_t)
        score_grad = (weights * (prob_grad - row_dot)).astype(jnp.bfloat16)
        dq = (dot_nn(kt, score_grad) * SCALE).astype(jnp.bfloat16).T
        joined_ref[block, 2 * TOK :] = dq
        dk_s[rows] += dot_nn(score_grad, q)
        dv_s[rows] += dot_nn(probs, grad)

    by_width(width_ref, block, attend)

    @pl.when(block == ROW - 1)
    def _():
        outs = (dkvh_ref, joined_ref, dkv_hi_ref)
        for b in range(SPAN + ROW):
            rows = slice(b * TOK, (b + 1) * TOK)
            ref = outs[b // SPAN]
            ref[b % SPAN, :TOK] = (dk_s[rows] * SCALE).astype(ref.dtype)
            ref[b % SPAN, TOK : 2 * TOK] = dv_s[rows].astype(ref.dtype)


KEYS = (SPAN + ROW) * TOK


def whole(*shape):
    return pl.BlockSpec(shape, lambda b, w: (0,) * len(shape))


def each(*shape):
    return pl.BlockSpec((1,) + shape, lambda b, w: (b, 0, 0))


SHARED_SPECS = [
    whole(ROW, 3 * TOK, HD),
    whole(SPAN, 2 * TOK, HD),
    whole(KEYS, HD),
    each(1, TOK),
    each(2 * TOK, HD),
]


def attention_fwd(widths, packed, kvh, kdoc, qdoc, qk):
    operands = [*hbm(packed, kvh), kdoc, qdoc, *hbm(qk)]
    return pl.pallas_call(
        fwd_kernel,
        grid_spec=pltpu.PrefetchScalarGridSpec(
            num_scalar_prefetch=1,
            grid=(ROW,),
            in_specs=SHARED_SPECS,
            out_specs=[each(TOK, HD), each(TOK, HD), each(1, TOK), each(1, TOK)],
            scratch_shapes=[
                pltpu.VMEM((KEYS, HD), jnp.bfloat16),
                pltpu.VMEM((SPAN + ROW, HD, TOK), jnp.bfloat16),
            ],
        ),
        out_shape=[
            pltpu.HBM((ROW, TOK, HD), jnp.bfloat16),
            pltpu.HBM((ROW, TOK, HD), jnp.bfloat16),
            jax.ShapeDtypeStruct((ROW, 1, TOK), jnp.float32),
            jax.ShapeDtypeStruct((ROW, 1, TOK), jnp.float32),
        ],
        compiler_params=pltpu.CompilerParams(vmem_limit_bytes=40 << 20),
        name="attn_fwd",
    )(widths, *operands)


def attention_bwd(widths, packed, kvh, kdoc, qdoc, qk, mixed_grad, out, top, inv):
    operands = [*hbm(packed, kvh), kdoc, qdoc, *hbm(qk, mixed_grad, out), top, inv]
    return pl.pallas_call(
        bwd_kernel,
        grid_spec=pltpu.PrefetchScalarGridSpec(
            num_scalar_prefetch=1,
            grid=(ROW,),
            in_specs=SHARED_SPECS + [each(TOK, HD), each(TOK, HD), each(1, TOK), each(1, TOK)],
            out_specs=[whole(ROW, 3 * TOK, HD)] + [whole(SPAN, 2 * TOK, HD)] * 2,
            scratch_shapes=[
                pltpu.VMEM((KEYS, HD), jnp.bfloat16),
                pltpu.VMEM((KEYS, HD), jnp.bfloat16),
                pltpu.VMEM((SPAN + ROW, HD, TOK), jnp.bfloat16),
                pltpu.VMEM((KEYS, HD), jnp.float32),
                pltpu.VMEM((KEYS, HD), jnp.float32),
            ],
        ),
        out_shape=[
            pltpu.HBM((ROW, 3 * TOK, HD), jnp.bfloat16),
            pltpu.HBM((SPAN, 2 * TOK, HD), jnp.float32),
            pltpu.HBM((SPAN, 2 * TOK, HD), jnp.bfloat16),
        ],
        compiler_params=pltpu.CompilerParams(vmem_limit_bytes=40 << 20),
        name="attn_bwd",
    )(widths, *operands)


def per_device(
    queries_in, keys_in, values_in, gate_branch, key_branch, mr_filter, out_grad, doc_ids
):
    n_seq = lax.axis_size("seq")
    position = lax.axis_index("seq")
    rings = [list(range(g, g + ROW)) for g in range(0, n_seq, ROW)]

    def swap(x, groups=rings, axis="seq"):
        return lax.all_to_all(x, axis, 0, 0, axis_index_groups=groups, tiled=True)

    def shift(x, by):
        pairs = [(i, i + by) for i in range(n_seq) if 0 <= i + by < n_seq]
        return lax.ppermute(x, "seq", pairs)

    doc_front = jnp.concatenate([jnp.full((SPAN * TOK,), -1, jnp.int32), doc_ids], 0)
    docs = lax.dynamic_slice_in_dim(
        doc_front, (position // ROW) * (ROW * TOK), (SPAN + ROW) * TOK, 0
    ).reshape(SPAN + ROW, TOK)
    widths = jnp.ones((ROW,), jnp.int32)
    for back in range(1, SPAN + 1):
        widths = widths + (docs[SPAN - back : SPAN + ROW - back, -1] == docs[SPAN:, 0])
    kdoc = jnp.broadcast_to(docs.reshape(-1, 1), ((SPAN + ROW) * TOK, HD))
    qdoc = docs[SPAN:].reshape(ROW, 1, TOK)

    conv_grad = (out_grad.astype(jnp.float32) * gate_branch.astype(jnp.float32)).astype(
        jnp.bfloat16
    )
    grad_edge = shift(conv_grad[:TAPS], -1)
    packed = swap(pack(conv_grad, keys_in, values_in))
    mixed_grad = anti_conv(
        jnp.concatenate([conv_grad, grad_edge[: TAPS - 1]], 0), mr_filter
    )
    qk = swap(pack(queries_in, key_branch))

    kvh = shift(packed[ROW - SPAN :, TOK:], ROW)
    head_edge = shift(packed[0, :TAPS], -ROW)
    head = position % ROW
    own_taps = lax.dynamic_slice_in_dim(mr_filter, head * HD, HD, 1)
    mixed_grad_head = head_anti(packed, head_edge, own_taps)

    shared = (widths, packed, kvh, kdoc, qdoc, qk)
    attn_head, mixed_head, top, inv = attention_fwd(*shared)
    attn_out = swap(attn_head)
    mixed_before = shift(mixed_head[ROW - 1, TOK - TAPS :], ROW)
    joined, dkv_hi, dkvh = attention_bwd(
        *shared, mixed_grad_head, attn_head, top, inv
    )
    back = shift(dkvh, -ROW)
    filter_part = head_corr(mixed_head, mixed_before, packed)
    mixed, branch_grad = finish(attn_out, key_branch, mixed_grad)
    mixed_edge = shift(mixed[TOK - TAPS :], 1)
    key_grad, value_grad, query_grad = unpack(swap(join(joined, dkv_hi, back)))
    gate_grad = []
    for piece in range(PIECES):
        gate_grad = [
            causal_piece(piece, mixed, mixed_edge, mr_filter, out_grad, gate_grad)
        ]
    gate_grad = gate_grad[0]

    def meet(x, axis, hop):
        pairs = [(i, i ^ hop) for i in range(lax.axis_size(axis))]
        return x + lax.ppermute(x, axis, pairs)

    rings_n = n_seq // ROW
    filter_grad = filter_part
    hop = ROW
    while hop < n_seq:
        filter_grad = meet(filter_grad, "seq", hop)
        hop *= 2
    tap_share = TAPS // ROW
    own_filter = lax.dynamic_slice_in_dim(mr_filter, head * tap_share, tap_share, 0)
    norms = jnp.stack(
        [jnp.sum(jnp.square(own_filter.astype(jnp.float32))), jnp.sum(filter_grad * filter_grad)]
    )
    norms = jnp.broadcast_to(norms[:, None], (2, HD))
    hop = 1
    while hop < lax.axis_size("ch"):
        norms = meet(norms, "ch", hop)
        hop *= 2
    tap_rows = TAPS // n_seq
    ring_taps = lax.dynamic_slice_in_dim(
        filter_grad, (position // ROW) * (TAPS // rings_n), TAPS // rings_n, 0
    ).reshape(ROW, tap_rows, HD)
    sent = jnp.concatenate([ring_taps, jnp.broadcast_to(norms[None], (ROW, 2, HD))], 1)
    got = swap(sent)
    own_grad = jnp.swapaxes(got[:, :tap_rows], 0, 1).reshape(tap_rows, ROW * HD)
    norms = jnp.sum(got[:, tap_rows:], 0)
    trust = jnp.sqrt(norms[0, 0]) / jnp.sqrt(norms[1, 0] + 1e-06)
    filter_step = trust * own_grad
    return (query_grad, key_grad, value_grad, gate_grad, branch_grad, filter_step)


def solution(mesh):
    rows = P("seq", "ch")
    return jax.shard_map(
        per_device,
        mesh=mesh,
        in_specs=(rows, rows, rows, rows, rows, P(None, "ch"), rows, P()),
        out_specs=(rows,) * 6,
        check_vma=False,
    )
```

```python
import jax
import jax.numpy as jnp
from jax import lax
from jax.experimental import pallas as pl
from jax.experimental.pallas import tpu as pltpu
from jax.sharding import PartitionSpec as P


HD = 128
TAPS = 128
SPAN = 4
ROW = 8
DOCS = 64
TOK = 256
EXT = TOK + TAPS
NEG = -1e30
STEP = 4
SCALE = HD ** (-0.5)
PIECES = 2


def hbm(*arrays):
    return [pltpu.with_memory_space_constraint(x, pltpu.HBM) for x in arrays]


def pack_kernel(*refs):
    *in_refs, out_ref = refs
    for head in range(out_ref.shape[0]):
        for n, in_ref in enumerate(in_refs):
            out_ref[head, n * TOK : (n + 1) * TOK] = in_ref[:, head * HD : (head + 1) * HD]


def pack(*arrays):
    heads = arrays[0].shape[1] // HD
    n = len(arrays)
    return pl.pallas_call(
        pack_kernel,
        grid=(heads // STEP,),
        in_specs=[pl.BlockSpec((TOK, STEP * HD), lambda h: (0, h))] * n,
        out_specs=pl.BlockSpec((STEP, n * TOK, HD), lambda h: (h, 0, 0)),
        out_shape=pltpu.HBM((heads, n * TOK, HD), arrays[0].dtype),
        name="pack",
    )(*arrays)


def unpack_kernel(x_ref, *out_refs):
    for head in range(x_ref.shape[0]):
        for n, out_ref in enumerate(out_refs):
            out_ref[:, head * HD : (head + 1) * HD] = x_ref[head, n * TOK : (n + 1) * TOK]


def unpack(x):
    heads, rows, _ = x.shape
    n = rows // TOK
    return pl.pallas_call(
        unpack_kernel,
        grid=(heads // STEP,),
        in_specs=[pl.BlockSpec((STEP, rows, HD), lambda h: (h, 0, 0))],
        out_specs=[pl.BlockSpec((TOK, STEP * HD), lambda h: (0, h))] * n,
        out_shape=[jax.ShapeDtypeStruct((TOK, heads * HD), x.dtype)] * n,
        name="unpack",
    )(*hbm(x))


def finish_kernel(x_ref, key_ref, mixed_grad_ref, mixed_ref, branch_ref):
    for head in range(x_ref.shape[0]):
        lanes = slice(head * HD, (head + 1) * HD)
        attn_out = x_ref[head].astype(jnp.float32)
        mixed_ref[:, lanes] = (key_ref[:, lanes].astype(jnp.float32) * attn_out).astype(
            jnp.bfloat16
        )
        branch_ref[:, lanes] = (mixed_grad_ref[:, lanes] * attn_out).astype(jnp.bfloat16)


def finish(attn_out, key, mixed_grad):
    heads = attn_out.shape[0]
    column = pl.BlockSpec((TOK, STEP * HD), lambda h: (0, h))
    shape = jax.ShapeDtypeStruct((TOK, heads * HD), jnp.bfloat16)
    return pl.pallas_call(
        finish_kernel,
        grid=(heads // STEP,),
        in_specs=[pl.BlockSpec((STEP, TOK, HD), lambda h: (h, 0, 0)), column, column],
        out_specs=[column] * 2,
        out_shape=[shape] * 2,
        name="finish",
    )(*hbm(attn_out), key, *hbm(mixed_grad))


def join_kernel(joined_ref, own_ref, back_ref, out_ref):
    out_ref[...] = (own_ref[...] + back_ref[...].astype(jnp.float32)).astype(jnp.bfloat16)


def join(joined, own, back):
    part = pl.BlockSpec((2, 2 * TOK, HD), lambda b: (b, 0, 0))
    first = (ROW - SPAN) // 2
    return pl.pallas_call(
        join_kernel,
        grid=(SPAN // 2,),
        in_specs=[pl.BlockSpec(memory_space=pl.ANY), part, part],
        out_specs=pl.BlockSpec((2, 2 * TOK, HD), lambda b: (b + first, 0, 0)),
        out_shape=pltpu.HBM(joined.shape, joined.dtype),
        input_output_aliases={0: 0},
        name="join",
    )(*hbm(joined, own, back))


def spread(tile_refs, ext_s, sh_s):
    at = 0
    for piece in tile_refs:
        ext_s[at : at + piece.shape[0]] = piece.astype(jnp.float32)
        at += piece.shape[0]
    ext_s[at:] = jnp.zeros((8, HD), jnp.float32)
    for r in range(8):
        sh_s[r] = ext_s[pl.ds(r, EXT)]


HALF = TOK // 2


def ahead(k, r):
    return r, k * 8


def behind(k, r):
    return ((8 - r) % 8, TAPS - 8 - k * 8) if r else (0, TAPS - k * 8)


def filtered(sh_s, w_s, where, half):
    def group(k, total):
        taps = w_s[pl.ds(pl.multiple_of(k * 8, 8), 8)]
        for r in range(8):
            slot, start = where(k, r)
            start = pl.multiple_of(start + half * HALF, 8)
            total = total + taps[r : r + 1] * sh_s[slot, pl.ds(start, HALF)]
        return total

    return lax.fori_loop(0, TAPS // 8, group, jnp.zeros((HALF, HD), jnp.float32))


def anti_kernel(g_ref, edge_ref, w_ref, out_ref, ext_s, sh_s, w_s):
    spread((g_ref[...], edge_ref[...]), ext_s, sh_s)
    w_s[...] = w_ref[...].astype(jnp.float32)
    for half in range(2):
        out_ref[half * HALF : (half + 1) * HALF] = filtered(sh_s, w_s, ahead, half)


def anti(conv_grad, edge, weights):
    column = lambda rows: pl.BlockSpec((rows, HD), lambda c: (0, c))
    return pl.pallas_call(
        anti_kernel,
        grid=(conv_grad.shape[1] // HD,),
        in_specs=[column(TOK), column(TAPS), column(TAPS)],
        out_specs=column(TOK),
        out_shape=pltpu.HBM(conv_grad.shape, jnp.float32),
        scratch_shapes=[
            pltpu.VMEM((EXT + 8, HD), jnp.float32),
            pltpu.VMEM((8, EXT, HD), jnp.float32),
            pltpu.VMEM((TAPS, HD), jnp.float32),
        ],
        name="anti",
    )(conv_grad, edge, weights)


def causal_kernel(m_ref, edge_ref, w_ref, grad_ref, *refs):
    out_ref, ext_s, sh_s, w_s = refs[-4:]
    spread((edge_ref[...], m_ref[...]), ext_s, sh_s)
    w_s[...] = w_ref[...].astype(jnp.float32)
    for half in range(2):
        rows = slice(half * HALF, (half + 1) * HALF)
        conv_out = filtered(sh_s, w_s, behind, half)
        out_ref[rows] = (grad_ref[rows].astype(jnp.float32) * conv_out).astype(jnp.bfloat16)


def causal_piece(piece, mixed, edge, weights, out_grad, before):
    tiles = mixed.shape[1] // HD // PIECES
    column = lambda rows: pl.BlockSpec((rows, HD), lambda c: (0, c + piece * tiles))
    return pl.pallas_call(
        causal_kernel,
        grid=(tiles,),
        in_specs=[column(TOK), column(TAPS), column(TAPS), column(TOK)]
        + [pl.BlockSpec(memory_space=pl.ANY)] * len(before),
        out_specs=column(TOK),
        out_shape=pltpu.HBM(mixed.shape, jnp.bfloat16),
        scratch_shapes=[
            pltpu.VMEM((EXT + 8, HD), jnp.float32),
            pltpu.VMEM((8, EXT, HD), jnp.float32),
            pltpu.VMEM((TAPS, HD), jnp.float32),
        ],
        input_output_aliases={4: 0} if before else {},
        name="causal",
    )(mixed, edge, weights, out_grad, *hbm(*before))


def head_anti_kernel(cur_ref, next_ref, edge_ref, w_ref, out_ref, ext_s, sh_s, w_s):
    last = pl.program_id(0) == ROW - 1
    after = jnp.where(last, edge_ref[...].astype(jnp.float32), next_ref[0].astype(jnp.float32))
    spread((cur_ref[0], after), ext_s, sh_s)
    w_s[...] = w_ref[...].astype(jnp.float32)
    for half in range(2):
        out_ref[0, half * HALF : (half + 1) * HALF] = filtered(sh_s, w_s, ahead, half)


def head_anti(packed, edge, weights):
    return pl.pallas_call(
        head_anti_kernel,
        grid=(ROW,),
        in_specs=[
            pl.BlockSpec((1, TOK, HD), lambda b: (b, 0, 0)),
            pl.BlockSpec((1, TAPS, HD), lambda b: (jnp.minimum(b + 1, ROW - 1), 0, 0)),
            pl.BlockSpec((TAPS, HD), lambda b: (0, 0)),
            pl.BlockSpec((TAPS, HD), lambda b: (0, 0)),
        ],
        out_specs=pl.BlockSpec((1, TOK, HD), lambda b: (b, 0, 0)),
        out_shape=pltpu.HBM((ROW, TOK, HD), jnp.float32),
        scratch_shapes=[
            pltpu.VMEM((EXT + 8, HD), jnp.float32),
            pltpu.VMEM((8, EXT, HD), jnp.float32),
            pltpu.VMEM((TAPS, HD), jnp.float32),
        ],
        name="head_anti",
    )(*hbm(packed, packed), edge, weights)


def head_corr_kernel(cur_ref, prev_ref, edge_ref, g_ref, out_ref, ext_s, sh_s, g_s, part_s):
    block = pl.program_id(0)
    before = jnp.where(
        block == 0, edge_ref[...].astype(jnp.float32), prev_ref[0].astype(jnp.float32)
    )
    spread((before, cur_ref[0]), ext_s, sh_s)
    g_s[...] = g_ref[0].astype(jnp.float32)

    @pl.when(block == 0)
    def _():
        part_s[...] = jnp.zeros_like(part_s)

    rows = TOK // 2

    def half_of(half, _):
        base = pl.multiple_of(half * rows, rows)
        g = [g_s[pl.ds(base + 8 * i, 8)] for i in range(rows // 8)]
        for r in range(8):
            for group in range(2):
                low = (72 if r == 0 else 64) - 64 * group
                piece = [
                    sh_s[(8 - r) % 8, pl.ds(base + low + 8 * i, 8)] for i in range(rows // 8 + 7)
                ]
                for kk in range(8):
                    total = g[0] * piece[7 - kk]
                    for i in range(1, rows // 8):
                        total = total + g[i] * piece[i + 7 - kk]
                    part_s[r, 8 * group + kk] += total
        return 0

    lax.fori_loop(0, 2, half_of, 0)

    @pl.when(block == ROW - 1)
    def _():
        for r in range(8):
            out_ref[pl.ds(r, TAPS // 8, stride=8)] = jnp.sum(part_s[r], 1)


def head_corr(mixed, edge, packed):
    return pl.pallas_call(
        head_corr_kernel,
        grid=(ROW,),
        in_specs=[
            pl.BlockSpec((1, TOK, HD), lambda b: (b, 0, 0)),
            pl.BlockSpec((1, TAPS, HD), lambda b: (jnp.maximum(b - 1, 0), 1, 0)),
            pl.BlockSpec((TAPS, HD), lambda b: (0, 0)),
            pl.BlockSpec((1, TOK, HD), lambda b: (b, 0, 0)),
        ],
        out_specs=pl.BlockSpec((TAPS, HD), lambda b: (0, 0)),
        out_shape=jax.ShapeDtypeStruct((TAPS, HD), jnp.float32),
        scratch_shapes=[
            pltpu.VMEM((EXT + 8, HD), jnp.float32),
            pltpu.VMEM((8, EXT, HD), jnp.float32),
            pltpu.VMEM((TOK, HD), jnp.float32),
            pltpu.VMEM((8, TAPS // 8, 8, HD), jnp.float32),
        ],
        name="head_corr",
    )(*hbm(mixed, mixed), edge, *hbm(packed))


def dot_nn(a, b):
    return jnp.dot(a, b, preferred_element_type=jnp.float32)


def norm_kernel(a_ref, b_ref, w_ref, sum_ref, norms_ref):
    total = a_ref[...] + b_ref[...]
    sum_ref[...] = total
    filter_sq = jnp.sum(jnp.square(w_ref[...].astype(jnp.float32)))
    norms_ref[...] = jnp.zeros_like(norms_ref)
    norms_ref[0:1] = jnp.full((1, HD), filter_sq, jnp.float32)
    norms_ref[1:2] = jnp.full((1, HD), jnp.sum(total * total), jnp.float32)


def norm_parts(a, b, weights):
    return pl.pallas_call(
        norm_kernel,
        out_shape=[
            jax.ShapeDtypeStruct(a.shape, jnp.float32),
            jax.ShapeDtypeStruct((8, HD), jnp.float32),
        ],
        name="norm_parts",
    )(a, b, weights)


def step_kernel(got_ref, out_ref):
    rows = out_ref.shape[0]
    norms = jnp.sum(got_ref[:, rows : rows + 2], 0)
    trust = jnp.sqrt(norms[0:1]) / jnp.sqrt(norms[1:2] + 1e-06)
    for head in range(ROW):
        out_ref[:, head * HD : (head + 1) * HD] = trust * got_ref[head, :rows]


def scaled_step(got, rows):
    return pl.pallas_call(
        step_kernel,
        out_shape=jax.ShapeDtypeStruct((rows, ROW * HD), jnp.float32),
        name="scaled_step",
    )(got)


def window_of(block, width):
    first = block + (SPAN + 1 - width)
    return first, pl.ds(pl.multiple_of(first * TOK, TOK), width * TOK)


def key_blocks(packed_ref, kvh_ref):
    for b in range(SPAN + ROW):
        src = kvh_ref if b < SPAN else packed_ref
        at = b if b < SPAN else b - SPAN
        skip = 0 if b < SPAN else TOK
        k = src[at, skip : skip + TOK]
        yield b, slice(b * TOK, (b + 1) * TOK), k, src[at, skip + TOK :]


def masked_scores(k, q, starts, first, width):
    scores = dot_nn(k, q.T)
    key_at = lax.broadcasted_iota(jnp.int32, scores.shape, 0)
    allowed = key_at >= starts - first * TOK
    own = (width - 1) * TOK
    query_at = lax.broadcasted_iota(jnp.int32, (TOK, TOK), 1)
    causal = allowed[own:] & (lax.broadcasted_iota(jnp.int32, (TOK, TOK), 0) <= query_at)
    diagonal = jnp.where(causal, scores[own:], NEG)
    if width == 1:
        return diagonal
    return jnp.concatenate([jnp.where(allowed[:own], scores[:own], NEG), diagonal], 0)


def each_block(width_ref, attend):
    def step(block, carry):
        for width in range(1, SPAN + 2):
            pl.when(width_ref[block] == width)(lambda width=width: attend(block, width))
        return carry

    lax.fori_loop(0, ROW, step, 0)


def fwd_kernel(
    width_ref, packed_ref, kvh_ref, starts_ref, qk_ref,
    out_ref, mixed_ref, top_ref, inv_ref, k_s, vt_s,
):
    for b, rows, k, v in key_blocks(packed_ref, kvh_ref):
        k_s[rows] = k
        vt_s[b] = v.T

    def attend(block, width):
        first, rows = window_of(block, width)
        q = qk_ref[block, :TOK]
        vt = jnp.concatenate([vt_s[first + n] for n in range(width)], 1)
        scores = masked_scores(k_s[rows], q, starts_ref[block], first, width)
        top = jnp.max(scores, 0, keepdims=True)
        weights = jnp.exp((scores - top) * SCALE)
        inv = 1.0 / jnp.sum(weights, 0, keepdims=True)
        top_ref[block] = top
        inv_ref[block] = inv
        probs = (weights * inv).astype(jnp.bfloat16)
        out = dot_nn(vt, probs).astype(jnp.bfloat16).T
        out_ref[block] = out
        key = qk_ref[block, TOK:].astype(jnp.float32)
        mixed_ref[block] = (key * out.astype(jnp.float32)).astype(jnp.bfloat16)

    each_block(width_ref, attend)


def bwd_kernel(
    width_ref, packed_ref, kvh_ref, starts_ref, qk_ref, mixed_grad_ref,
    out_ref, top_ref, inv_ref,
    joined_ref, dkv_hi_ref, dkvh_ref, k_s, v_s, kt_s, dk_s, dv_s,
):
    for b, rows, k, v in key_blocks(packed_ref, kvh_ref):
        k_s[rows] = k
        v_s[rows] = v
        kt_s[b] = k.T
    dk_s[...] = jnp.zeros_like(dk_s)
    dv_s[...] = jnp.zeros_like(dv_s)

    def attend(block, width):
        first, rows = window_of(block, width)
        q = qk_ref[block, :TOK]
        key = qk_ref[block, TOK:].astype(jnp.float32)
        grad = (mixed_grad_ref[block] * key).astype(jnp.bfloat16)
        grad_t = grad.T
        kt = jnp.concatenate([kt_s[first + n] for n in range(width)], 1)
        scores = masked_scores(k_s[rows], q, starts_ref[block], first, width)
        weights = jnp.exp((scores - top_ref[block]) * SCALE) * inv_ref[block]
        probs = weights.astype(jnp.bfloat16)
        row_dot = jnp.sum(
            out_ref[block].T.astype(jnp.float32) * grad_t.astype(jnp.float32), 0, keepdims=True
        )
        prob_grad = dot_nn(v_s[rows], grad_t)
        score_grad = (weights * (prob_grad - row_dot)).astype(jnp.bfloat16)
        dq = (dot_nn(kt, score_grad) * SCALE).astype(jnp.bfloat16).T
        joined_ref[block, 2 * TOK :] = dq
        dk_s[rows] += dot_nn(score_grad, q)
        dv_s[rows] += dot_nn(probs, grad)

    each_block(width_ref, attend)
    outs = (dkvh_ref, joined_ref, dkv_hi_ref)
    for b in range(SPAN + ROW):
        rows = slice(b * TOK, (b + 1) * TOK)
        ref = outs[b // SPAN]
        ref[b % SPAN, :TOK] = (dk_s[rows] * SCALE).astype(ref.dtype)
        ref[b % SPAN, TOK : 2 * TOK] = dv_s[rows].astype(ref.dtype)


KEYS = (SPAN + ROW) * TOK


def whole(*shape):
    return pl.BlockSpec(shape, lambda b, w: (0,) * len(shape))


TOKEN_SPEC = whole(ROW, TOK, HD)
STAT_SPEC = whole(ROW, 1, TOK)
SHARED_SPECS = [
    whole(ROW, 3 * TOK, HD),
    whole(SPAN, 2 * TOK, HD),
    STAT_SPEC,
    whole(ROW, 2 * TOK, HD),
]


def attention_fwd(widths, packed, kvh, starts, qk):
    operands = [*hbm(packed, kvh), starts, *hbm(qk)]
    return pl.pallas_call(
        fwd_kernel,
        grid_spec=pltpu.PrefetchScalarGridSpec(
            num_scalar_prefetch=1,
            grid=(1,),
            in_specs=SHARED_SPECS,
            out_specs=[TOKEN_SPEC, TOKEN_SPEC, STAT_SPEC, STAT_SPEC],
            scratch_shapes=[
                pltpu.VMEM((KEYS, HD), jnp.bfloat16),
                pltpu.VMEM((SPAN + ROW, HD, TOK), jnp.bfloat16),
            ],
        ),
        out_shape=[
            pltpu.HBM((ROW, TOK, HD), jnp.bfloat16),
            pltpu.HBM((ROW, TOK, HD), jnp.bfloat16),
            jax.ShapeDtypeStruct((ROW, 1, TOK), jnp.float32),
            jax.ShapeDtypeStruct((ROW, 1, TOK), jnp.float32),
        ],
        compiler_params=pltpu.CompilerParams(vmem_limit_bytes=40 << 20),
        name="attn_fwd",
    )(widths, *operands)


def attention_bwd(widths, packed, kvh, starts, qk, mixed_grad, out, top, inv):
    operands = [*hbm(packed, kvh), starts, *hbm(qk, mixed_grad, out), top, inv]
    return pl.pallas_call(
        bwd_kernel,
        grid_spec=pltpu.PrefetchScalarGridSpec(
            num_scalar_prefetch=1,
            grid=(1,),
            in_specs=SHARED_SPECS + [TOKEN_SPEC, TOKEN_SPEC, STAT_SPEC, STAT_SPEC],
            out_specs=[whole(ROW, 3 * TOK, HD)] + [whole(SPAN, 2 * TOK, HD)] * 2,
            scratch_shapes=[
                pltpu.VMEM((KEYS, HD), jnp.bfloat16),
                pltpu.VMEM((KEYS, HD), jnp.bfloat16),
                pltpu.VMEM((SPAN + ROW, HD, TOK), jnp.bfloat16),
                pltpu.VMEM((KEYS, HD), jnp.float32),
                pltpu.VMEM((KEYS, HD), jnp.float32),
            ],
        ),
        out_shape=[
            pltpu.HBM((ROW, 3 * TOK, HD), jnp.bfloat16),
            pltpu.HBM((SPAN, 2 * TOK, HD), jnp.float32),
            pltpu.HBM((SPAN, 2 * TOK, HD), jnp.bfloat16),
        ],
        compiler_params=pltpu.CompilerParams(vmem_limit_bytes=40 << 20),
        name="attn_bwd",
    )(widths, *operands)


def per_device(
    queries_in, keys_in, values_in, gate_branch, key_branch, mr_filter, out_grad, doc_ids
):
    n_seq = lax.axis_size("seq")
    position = lax.axis_index("seq")
    rings = [list(range(g, g + ROW)) for g in range(0, n_seq, ROW)]

    def swap(x, groups=rings, axis="seq"):
        return lax.all_to_all(x, axis, 0, 0, axis_index_groups=groups, tiled=True)

    def shift(x, by):
        pairs = [(i, i + by) for i in range(n_seq) if 0 <= i + by < n_seq]
        return lax.ppermute(x, "seq", pairs)

    doc_front = jnp.concatenate([jnp.full((SPAN * TOK,), -1, jnp.int32), doc_ids], 0)
    docs = lax.dynamic_slice_in_dim(
        doc_front, (position // ROW) * (ROW * TOK), (SPAN + ROW) * TOK, 0
    ).reshape(SPAN + ROW, TOK)
    widths = jnp.ones((ROW,), jnp.int32)
    for back in range(1, SPAN + 1):
        widths = widths + (docs[SPAN - back : SPAN + ROW - back, -1] == docs[SPAN:, 0])
    numbers = jnp.arange(DOCS, dtype=jnp.int32)[:, None]
    first_rows = jnp.sum((doc_ids[None] < numbers).astype(jnp.int32), 1, keepdims=True)
    first_rows = first_rows - ((position // ROW) * ROW - SPAN) * TOK
    starts = jnp.sum(jnp.where(docs[SPAN:].reshape(1, -1) == numbers, first_rows, 0), 0)
    starts = starts.reshape(ROW, 1, TOK)

    conv_grad = (out_grad.astype(jnp.float32) * gate_branch.astype(jnp.float32)).astype(
        jnp.bfloat16
    )
    grad_edge = shift(conv_grad[:TAPS], -1)
    packed = swap(pack(conv_grad, keys_in, values_in))
    mixed_grad = anti(conv_grad, grad_edge, mr_filter)
    qk = swap(pack(queries_in, key_branch))

    kvh = shift(packed[ROW - SPAN :, TOK:], ROW)
    head_edge = shift(packed[0, :TAPS], -ROW)
    head = position % ROW
    own_taps = lax.dynamic_slice_in_dim(mr_filter, head * HD, HD, 1)
    mixed_grad_head = head_anti(packed, head_edge, own_taps)

    shared = (widths, packed, kvh, starts, qk)
    attn_head, mixed_head, top, inv = attention_fwd(*shared)
    attn_out = swap(attn_head)
    mixed_before = shift(mixed_head[ROW - 1, TOK - TAPS :], ROW)
    joined, dkv_hi, dkvh = attention_bwd(
        *shared, mixed_grad_head, attn_head, top, inv
    )
    back = shift(dkvh, -ROW)
    filter_part = head_corr(mixed_head, mixed_before, packed)
    mixed, branch_grad = finish(attn_out, key_branch, mixed_grad)
    mixed_edge = shift(mixed[TOK - TAPS :], 1)
    key_grad, value_grad, query_grad = unpack(swap(join(joined, dkv_hi, back)))
    gate_grad = []
    for piece in range(PIECES):
        gate_grad = [
            causal_piece(piece, mixed, mixed_edge, mr_filter, out_grad, gate_grad)
        ]
    gate_grad = gate_grad[0]

    def partner(x, axis, hop):
        pairs = [(i, i ^ hop) for i in range(lax.axis_size(axis))]
        return lax.ppermute(x, axis, pairs)

    rings_n = n_seq // ROW
    tap_share = TAPS // ROW
    own_filter = lax.dynamic_slice_in_dim(mr_filter, head * tap_share, tap_share, 0)
    filter_grad = filter_part + partner(filter_part, "seq", ROW)
    other = partner(filter_grad, "seq", 2 * ROW)
    filter_grad, norms = norm_parts(filter_grad, other, own_filter)
    hop = 1
    while hop < lax.axis_size("ch"):
        norms = norms + partner(norms, "ch", hop)
        hop *= 2
    tap_rows = TAPS // n_seq
    ring_taps = lax.dynamic_slice_in_dim(
        filter_grad, (position // ROW) * (TAPS // rings_n), TAPS // rings_n, 0
    ).reshape(ROW, tap_rows, HD)
    spread_norms = jnp.broadcast_to(norms[None, :tap_rows], (ROW, tap_rows, HD))
    got = swap(jnp.concatenate([ring_taps, spread_norms], 1))
    filter_step = scaled_step(got, tap_rows)
    return (query_grad, key_grad, value_grad, gate_grad, branch_grad, filter_step)


def solution(mesh):
    rows = P("seq", "ch")
    return jax.shard_map(
        per_device,
        mesh=mesh,
        in_specs=(rows, rows, rows, rows, rows, P(None, "ch"), rows, P()),
        out_specs=(rows,) * 6,
        check_vma=False,
    )
```

```python
import jax
import jax.numpy as jnp
from jax import lax
from jax.experimental import pallas as pl
from jax.experimental.pallas import tpu as pltpu
from jax.sharding import PartitionSpec as P


HD = 128
TAPS = 128
SPAN = 4
ROW = 8
DOCS = 64
TOK = 256
EXT = TOK + TAPS
NEG = -1e30
GRANT = pltpu.CompilerParams(vmem_limit_bytes=8 << 20)
STEP = 4
SCALE = HD ** (-0.5)
PIECES = 2


def hbm(*arrays):
    return [pltpu.with_memory_space_constraint(x, pltpu.HBM) for x in arrays]


def pack_kernel(*refs):
    *in_refs, out_ref = refs
    for head in range(out_ref.shape[0]):
        for n, in_ref in enumerate(in_refs):
            out_ref[head, n * TOK : (n + 1) * TOK] = in_ref[:, head * HD : (head + 1) * HD]


def pack(*arrays):
    heads = arrays[0].shape[1] // HD
    n = len(arrays)
    return pl.pallas_call(
        pack_kernel,
        grid=(heads // STEP,),
        in_specs=[pl.BlockSpec((TOK, STEP * HD), lambda h: (0, h))] * n,
        out_specs=pl.BlockSpec((STEP, n * TOK, HD), lambda h: (h, 0, 0)),
        out_shape=pltpu.HBM((heads, n * TOK, HD), arrays[0].dtype),
        compiler_params=GRANT,
        name="pack",
    )(*arrays)


def unpack_kernel(x_ref, *out_refs):
    for head in range(x_ref.shape[0]):
        for n, out_ref in enumerate(out_refs):
            out_ref[:, head * HD : (head + 1) * HD] = x_ref[head, n * TOK : (n + 1) * TOK]


def unpack(x):
    heads, rows, _ = x.shape
    n = rows // TOK
    return pl.pallas_call(
        unpack_kernel,
        grid=(heads // STEP,),
        in_specs=[pl.BlockSpec((STEP, rows, HD), lambda h: (h, 0, 0))],
        out_specs=[pl.BlockSpec((TOK, STEP * HD), lambda h: (0, h))] * n,
        out_shape=[jax.ShapeDtypeStruct((TOK, heads * HD), x.dtype)] * n,
        compiler_params=GRANT,
        name="unpack",
    )(x)


def finish_kernel(x_ref, key_ref, mixed_grad_ref, mixed_ref, branch_ref):
    for head in range(x_ref.shape[0]):
        lanes = slice(head * HD, (head + 1) * HD)
        attn_out = x_ref[head].astype(jnp.float32)
        mixed_ref[:, lanes] = (key_ref[:, lanes].astype(jnp.float32) * attn_out).astype(
            jnp.bfloat16
        )
        branch_ref[:, lanes] = (mixed_grad_ref[:, lanes] * attn_out).astype(jnp.bfloat16)


def finish(attn_out, key, mixed_grad):
    heads = attn_out.shape[0]
    column = pl.BlockSpec((TOK, STEP * HD), lambda h: (0, h))
    shape = jax.ShapeDtypeStruct((TOK, heads * HD), jnp.bfloat16)
    return pl.pallas_call(
        finish_kernel,
        grid=(heads // STEP,),
        in_specs=[pl.BlockSpec((STEP, TOK, HD), lambda h: (h, 0, 0)), column, column],
        out_specs=[column] * 2,
        out_shape=[shape] * 2,
        compiler_params=GRANT,
        name="finish",
    )(attn_out, key, mixed_grad)


def join_kernel(joined_ref, own_ref, back_ref, out_ref):
    out_ref[...] = (own_ref[...] + back_ref[...].astype(jnp.float32)).astype(jnp.bfloat16)


def join(joined, own, back):
    part = pl.BlockSpec((2, 2 * TOK, HD), lambda b: (b, 0, 0))
    first = (ROW - SPAN) // 2
    return pl.pallas_call(
        join_kernel,
        grid=(SPAN // 2,),
        in_specs=[pl.BlockSpec(memory_space=pl.ANY), part, part],
        out_specs=pl.BlockSpec((2, 2 * TOK, HD), lambda b: (b + first, 0, 0)),
        out_shape=pltpu.HBM(joined.shape, joined.dtype),
        input_output_aliases={0: 0},
        compiler_params=GRANT,
        name="join",
    )(*hbm(joined), own, back)


def spread(tile_refs, ext_s, sh_s):
    at = 0
    for piece in tile_refs:
        ext_s[at : at + piece.shape[0]] = piece.astype(jnp.float32)
        at += piece.shape[0]
    ext_s[at:] = jnp.zeros((8, HD), jnp.float32)
    for r in range(8):
        sh_s[r] = ext_s[pl.ds(r, EXT)]


HALF = TOK // 2


def ahead(k, r):
    return r, k * 8


def behind(k, r):
    return ((8 - r) % 8, TAPS - 8 - k * 8) if r else (0, TAPS - k * 8)


def filtered(sh_s, w_s, where, half):
    def group(k, total):
        taps = w_s[pl.ds(pl.multiple_of(k * 8, 8), 8)]
        for r in range(8):
            slot, start = where(k, r)
            start = pl.multiple_of(start + half * HALF, 8)
            total = total + taps[r : r + 1] * sh_s[slot, pl.ds(start, HALF)]
        return total

    return lax.fori_loop(0, TAPS // 8, group, jnp.zeros((HALF, HD), jnp.float32))


def anti_kernel(g_ref, edge_ref, w_ref, out_ref, ext_s, sh_s, w_s):
    spread((g_ref[...], edge_ref[...]), ext_s, sh_s)
    w_s[...] = w_ref[...].astype(jnp.float32)
    for half in range(2):
        out_ref[half * HALF : (half + 1) * HALF] = filtered(sh_s, w_s, ahead, half)


def anti(conv_grad, edge, weights):
    column = lambda rows: pl.BlockSpec((rows, HD), lambda c: (0, c))
    return pl.pallas_call(
        anti_kernel,
        grid=(conv_grad.shape[1] // HD,),
        in_specs=[column(TOK), column(TAPS), column(TAPS)],
        out_specs=column(TOK),
        out_shape=jax.ShapeDtypeStruct(conv_grad.shape, jnp.float32),
        scratch_shapes=[
            pltpu.VMEM((EXT + 8, HD), jnp.float32),
            pltpu.VMEM((8, EXT, HD), jnp.float32),
            pltpu.VMEM((TAPS, HD), jnp.float32),
        ],
        compiler_params=GRANT,
        name="anti",
    )(conv_grad, edge, weights)


def causal_kernel(m_ref, edge_ref, w_ref, grad_ref, *refs):
    out_ref, ext_s, sh_s, w_s = refs[-4:]
    spread((edge_ref[...], m_ref[...]), ext_s, sh_s)
    w_s[...] = w_ref[...].astype(jnp.float32)
    for half in range(2):
        rows = slice(half * HALF, (half + 1) * HALF)
        conv_out = filtered(sh_s, w_s, behind, half)
        out_ref[rows] = (grad_ref[rows].astype(jnp.float32) * conv_out).astype(jnp.bfloat16)


def causal_piece(piece, mixed, edge, weights, out_grad, before):
    tiles = mixed.shape[1] // HD // PIECES
    column = lambda rows: pl.BlockSpec((rows, HD), lambda c: (0, c + piece * tiles))
    return pl.pallas_call(
        causal_kernel,
        grid=(tiles,),
        in_specs=[column(TOK), column(TAPS), column(TAPS), column(TOK)]
        + [pl.BlockSpec(memory_space=pl.ANY)] * len(before),
        out_specs=column(TOK),
        out_shape=pltpu.HBM(mixed.shape, jnp.bfloat16),
        scratch_shapes=[
            pltpu.VMEM((EXT + 8, HD), jnp.float32),
            pltpu.VMEM((8, EXT, HD), jnp.float32),
            pltpu.VMEM((TAPS, HD), jnp.float32),
        ],
        input_output_aliases={4: 0} if before else {},
        compiler_params=GRANT,
        name="causal",
    )(mixed, edge, weights, out_grad, *hbm(*before))


def head_anti_kernel(cur_ref, next_ref, edge_ref, w_ref, out_ref, ext_s, sh_s, w_s):
    last = pl.program_id(0) == ROW - 1
    after = jnp.where(last, edge_ref[...].astype(jnp.float32), next_ref[0].astype(jnp.float32))
    spread((cur_ref[0], after), ext_s, sh_s)
    w_s[...] = w_ref[...].astype(jnp.float32)
    for half in range(2):
        out_ref[0, half * HALF : (half + 1) * HALF] = filtered(sh_s, w_s, ahead, half)


def head_anti(packed, edge, weights):
    return pl.pallas_call(
        head_anti_kernel,
        grid=(ROW,),
        in_specs=[
            pl.BlockSpec((1, TOK, HD), lambda b: (b, 0, 0)),
            pl.BlockSpec((1, TAPS, HD), lambda b: (jnp.minimum(b + 1, ROW - 1), 0, 0)),
            pl.BlockSpec((TAPS, HD), lambda b: (0, 0)),
            pl.BlockSpec((TAPS, HD), lambda b: (0, 0)),
        ],
        out_specs=pl.BlockSpec((1, TOK, HD), lambda b: (b, 0, 0)),
        out_shape=jax.ShapeDtypeStruct((ROW, TOK, HD), jnp.float32),
        scratch_shapes=[
            pltpu.VMEM((EXT + 8, HD), jnp.float32),
            pltpu.VMEM((8, EXT, HD), jnp.float32),
            pltpu.VMEM((TAPS, HD), jnp.float32),
        ],
        compiler_params=GRANT,
        name="head_anti",
    )(packed, packed, edge, weights)


def head_corr_kernel(cur_ref, prev_ref, edge_ref, g_ref, out_ref, ext_s, sh_s, g_s, part_s):
    block = pl.program_id(0)
    before = jnp.where(
        block == 0, edge_ref[...].astype(jnp.float32), prev_ref[0].astype(jnp.float32)
    )
    spread((before, cur_ref[0]), ext_s, sh_s)
    g_s[...] = g_ref[0].astype(jnp.float32)

    @pl.when(block == 0)
    def _():
        part_s[...] = jnp.zeros_like(part_s)

    rows = TOK // 2

    def half_of(half, _):
        base = pl.multiple_of(half * rows, rows)
        g = [g_s[pl.ds(base + 8 * i, 8)] for i in range(rows // 8)]
        for r in range(8):
            for group in range(2):
                low = (72 if r == 0 else 64) - 64 * group
                piece = [
                    sh_s[(8 - r) % 8, pl.ds(base + low + 8 * i, 8)] for i in range(rows // 8 + 7)
                ]
                for kk in range(8):
                    total = g[0] * piece[7 - kk]
                    for i in range(1, rows // 8):
                        total = total + g[i] * piece[i + 7 - kk]
                    part_s[r, 8 * group + kk] += total
        return 0

    lax.fori_loop(0, 2, half_of, 0)

    @pl.when(block == ROW - 1)
    def _():
        for r in range(8):
            out_ref[pl.ds(r, TAPS // 8, stride=8)] = jnp.sum(part_s[r], 1)


def head_corr(mixed, edge, packed):
    return pl.pallas_call(
        head_corr_kernel,
        grid=(ROW,),
        in_specs=[
            pl.BlockSpec((1, TOK, HD), lambda b: (b, 0, 0)),
            pl.BlockSpec((1, TAPS, HD), lambda b: (jnp.maximum(b - 1, 0), 1, 0)),
            pl.BlockSpec((TAPS, HD), lambda b: (0, 0)),
            pl.BlockSpec((1, TOK, HD), lambda b: (b, 0, 0)),
        ],
        out_specs=pl.BlockSpec((TAPS, HD), lambda b: (0, 0)),
        out_shape=jax.ShapeDtypeStruct((TAPS, HD), jnp.float32),
        scratch_shapes=[
            pltpu.VMEM((EXT + 8, HD), jnp.float32),
            pltpu.VMEM((8, EXT, HD), jnp.float32),
            pltpu.VMEM((TOK, HD), jnp.float32),
            pltpu.VMEM((8, TAPS // 8, 8, HD), jnp.float32),
        ],
        compiler_params=GRANT,
        name="head_corr",
    )(mixed, mixed, edge, packed)


def dot_nn(a, b):
    return jnp.dot(a, b, preferred_element_type=jnp.float32)


def norm_kernel(a_ref, b_ref, w_ref, sum_ref, norms_ref):
    total = a_ref[...] + b_ref[...]
    sum_ref[...] = total
    filter_sq = jnp.sum(jnp.square(w_ref[...].astype(jnp.float32)))
    norms_ref[...] = jnp.zeros_like(norms_ref)
    norms_ref[0:1] = jnp.full((1, HD), filter_sq, jnp.float32)
    norms_ref[1:2] = jnp.full((1, HD), jnp.sum(total * total), jnp.float32)


def norm_parts(a, b, weights):
    return pl.pallas_call(
        norm_kernel,
        out_shape=[
            jax.ShapeDtypeStruct(a.shape, jnp.float32),
            jax.ShapeDtypeStruct((8, HD), jnp.float32),
        ],
        compiler_params=GRANT,
        name="norm_parts",
    )(a, b, weights)


def step_kernel(got_ref, out_ref):
    rows = out_ref.shape[0]
    norms = jnp.sum(got_ref[:, rows : rows + 2], 0)
    trust = jnp.sqrt(norms[0:1]) / jnp.sqrt(norms[1:2] + 1e-06)
    for head in range(ROW):
        out_ref[:, head * HD : (head + 1) * HD] = trust * got_ref[head, :rows]


def scaled_step(got, rows):
    return pl.pallas_call(
        step_kernel,
        out_shape=jax.ShapeDtypeStruct((rows, ROW * HD), jnp.float32),
        compiler_params=GRANT,
        name="scaled_step",
    )(got)


def window_of(block, width):
    first = block + (SPAN + 1 - width)
    return first, pl.ds(pl.multiple_of(first * TOK, TOK), width * TOK)


def key_blocks(packed_ref, kvh_ref):
    for b in range(SPAN + ROW):
        src = kvh_ref if b < SPAN else packed_ref
        at = b if b < SPAN else b - SPAN
        skip = 0 if b < SPAN else TOK
        k = src[at, skip : skip + TOK]
        yield b, slice(b * TOK, (b + 1) * TOK), k, src[at, skip + TOK :]


def masked_scores(k, q, starts, first, width):
    scores = dot_nn(k, q.T)
    key_at = lax.broadcasted_iota(jnp.int32, scores.shape, 0)
    allowed = key_at >= starts - first * TOK
    own = (width - 1) * TOK
    query_at = lax.broadcasted_iota(jnp.int32, (TOK, TOK), 1)
    causal = allowed[own:] & (lax.broadcasted_iota(jnp.int32, (TOK, TOK), 0) <= query_at)
    diagonal = jnp.where(causal, scores[own:], NEG)
    if width == 1:
        return diagonal
    return jnp.concatenate([jnp.where(allowed[:own], scores[:own], NEG), diagonal], 0)


def each_block(width_ref, attend):
    def step(block, carry):
        for width in range(1, SPAN + 2):
            pl.when(width_ref[block] == width)(lambda width=width: attend(block, width))
        return carry

    lax.fori_loop(0, ROW, step, 0)


def fwd_kernel(
    width_ref, packed_ref, kvh_ref, starts_ref, qk_ref,
    out_ref, mixed_ref, top_ref, inv_ref, k_s, vt_s,
):
    for b, rows, k, v in key_blocks(packed_ref, kvh_ref):
        k_s[rows] = k
        vt_s[b] = v.T

    def attend(block, width):
        first, rows = window_of(block, width)
        q = qk_ref[block, :TOK]
        vt = jnp.concatenate([vt_s[first + n] for n in range(width)], 1)
        scores = masked_scores(k_s[rows], q, starts_ref[block], first, width)
        top = jnp.max(scores, 0, keepdims=True)
        weights = jnp.exp((scores - top) * SCALE)
        inv = 1.0 / jnp.sum(weights, 0, keepdims=True)
        top_ref[block] = top
        inv_ref[block] = inv
        probs = (weights * inv).astype(jnp.bfloat16)
        out = dot_nn(vt, probs).astype(jnp.bfloat16).T
        out_ref[block] = out
        key = qk_ref[block, TOK:].astype(jnp.float32)
        mixed_ref[block] = (key * out.astype(jnp.float32)).astype(jnp.bfloat16)

    each_block(width_ref, attend)


def bwd_kernel(
    width_ref, packed_ref, kvh_ref, starts_ref, qk_ref, mixed_grad_ref,
    out_ref, top_ref, inv_ref,
    joined_ref, dkv_hi_ref, dkvh_ref, k_s, v_s, kt_s, dk_s, dv_s,
):
    for b, rows, k, v in key_blocks(packed_ref, kvh_ref):
        k_s[rows] = k
        v_s[rows] = v
        kt_s[b] = k.T
    dk_s[...] = jnp.zeros_like(dk_s)
    dv_s[...] = jnp.zeros_like(dv_s)

    def attend(block, width):
        first, rows = window_of(block, width)
        q = qk_ref[block, :TOK]
        key = qk_ref[block, TOK:].astype(jnp.float32)
        grad = (mixed_grad_ref[block] * key).astype(jnp.bfloat16)
        grad_t = grad.T
        kt = jnp.concatenate([kt_s[first + n] for n in range(width)], 1)
        scores = masked_scores(k_s[rows], q, starts_ref[block], first, width)
        weights = jnp.exp((scores - top_ref[block]) * SCALE) * inv_ref[block]
        probs = weights.astype(jnp.bfloat16)
        row_dot = jnp.sum(
            out_ref[block].T.astype(jnp.float32) * grad_t.astype(jnp.float32), 0, keepdims=True
        )
        prob_grad = dot_nn(v_s[rows], grad_t)
        score_grad = (weights * (prob_grad - row_dot)).astype(jnp.bfloat16)
        dq = (dot_nn(kt, score_grad) * SCALE).astype(jnp.bfloat16).T
        joined_ref[block, 2 * TOK :] = dq
        dk_s[rows] += dot_nn(score_grad, q)
        dv_s[rows] += dot_nn(probs, grad)

    each_block(width_ref, attend)
    outs = (dkvh_ref, joined_ref, dkv_hi_ref)
    for b in range(SPAN + ROW):
        rows = slice(b * TOK, (b + 1) * TOK)
        ref = outs[b // SPAN]
        ref[b % SPAN, :TOK] = (dk_s[rows] * SCALE).astype(ref.dtype)
        ref[b % SPAN, TOK : 2 * TOK] = dv_s[rows].astype(ref.dtype)


KEYS = (SPAN + ROW) * TOK


def whole(*shape):
    return pl.BlockSpec(shape, lambda b, w: (0,) * len(shape))


VMEM = pl.BlockSpec(memory_space=pltpu.VMEM)


def attention_fwd(widths, packed, kvh, starts, qk):
    operands = [packed, kvh, starts, qk]
    return pl.pallas_call(
        fwd_kernel,
        grid_spec=pltpu.PrefetchScalarGridSpec(
            num_scalar_prefetch=1,
            grid=(1,),
            in_specs=[VMEM] * 4,
            out_specs=[whole(ROW, TOK, HD), VMEM, VMEM, VMEM],
            scratch_shapes=[
                pltpu.VMEM((KEYS, HD), jnp.bfloat16),
                pltpu.VMEM((SPAN + ROW, HD, TOK), jnp.bfloat16),
            ],
        ),
        out_shape=[
            pltpu.HBM((ROW, TOK, HD), jnp.bfloat16),
            jax.ShapeDtypeStruct((ROW, TOK, HD), jnp.bfloat16),
            jax.ShapeDtypeStruct((ROW, 1, TOK), jnp.float32),
            jax.ShapeDtypeStruct((ROW, 1, TOK), jnp.float32),
        ],
        compiler_params=pltpu.CompilerParams(vmem_limit_bytes=20 << 20),
        name="attn_fwd",
    )(widths, *operands)


def attention_bwd(widths, packed, kvh, starts, qk, mixed_grad, out, top, inv):
    operands = [packed, kvh, starts, qk, mixed_grad, out, top, inv]
    return pl.pallas_call(
        bwd_kernel,
        grid_spec=pltpu.PrefetchScalarGridSpec(
            num_scalar_prefetch=1,
            grid=(1,),
            in_specs=[VMEM] * 8,
            out_specs=[whole(ROW, 3 * TOK, HD), VMEM, VMEM],
            scratch_shapes=[
                pltpu.VMEM((KEYS, HD), jnp.bfloat16),
                pltpu.VMEM((KEYS, HD), jnp.bfloat16),
                pltpu.VMEM((SPAN + ROW, HD, TOK), jnp.bfloat16),
                pltpu.VMEM((KEYS, HD), jnp.float32),
                pltpu.VMEM((KEYS, HD), jnp.float32),
            ],
        ),
        out_shape=[
            pltpu.HBM((ROW, 3 * TOK, HD), jnp.bfloat16),
            jax.ShapeDtypeStruct((SPAN, 2 * TOK, HD), jnp.float32),
            jax.ShapeDtypeStruct((SPAN, 2 * TOK, HD), jnp.bfloat16),
        ],
        compiler_params=pltpu.CompilerParams(vmem_limit_bytes=28 << 20),
        name="attn_bwd",
    )(widths, *operands)


def per_device(
    queries_in, keys_in, values_in, gate_branch, key_branch, mr_filter, out_grad, doc_ids
):
    n_seq = lax.axis_size("seq")
    position = lax.axis_index("seq")
    rings = [list(range(g, g + ROW)) for g in range(0, n_seq, ROW)]

    def swap(x, groups=rings, axis="seq"):
        return lax.all_to_all(x, axis, 0, 0, axis_index_groups=groups, tiled=True)

    def shift(x, by):
        pairs = [(i, i + by) for i in range(n_seq) if 0 <= i + by < n_seq]
        return lax.ppermute(x, "seq", pairs)

    doc_front = jnp.concatenate([jnp.full((SPAN * TOK,), -1, jnp.int32), doc_ids], 0)
    docs = lax.dynamic_slice_in_dim(
        doc_front, (position // ROW) * (ROW * TOK), (SPAN + ROW) * TOK, 0
    ).reshape(SPAN + ROW, TOK)
    widths = jnp.ones((ROW,), jnp.int32)
    for back in range(1, SPAN + 1):
        widths = widths + (docs[SPAN - back : SPAN + ROW - back, -1] == docs[SPAN:, 0])
    numbers = jnp.arange(DOCS, dtype=jnp.int32)[:, None]
    first_rows = jnp.sum((doc_ids[None] < numbers).astype(jnp.int32), 1, keepdims=True)
    first_rows = first_rows - ((position // ROW) * ROW - SPAN) * TOK
    starts = jnp.sum(jnp.where(docs[SPAN:].reshape(1, -1) == numbers, first_rows, 0), 0)
    starts = starts.reshape(ROW, 1, TOK)

    conv_grad = (out_grad.astype(jnp.float32) * gate_branch.astype(jnp.float32)).astype(
        jnp.bfloat16
    )
    grad_edge = shift(conv_grad[:TAPS], -1)
    packed = swap(pack(conv_grad, keys_in, values_in))
    mixed_grad = anti(conv_grad, grad_edge, mr_filter)
    qk = swap(pack(queries_in, key_branch))

    kvh = shift(packed[ROW - SPAN :, TOK:], ROW)
    head_edge = shift(packed[0, :TAPS], -ROW)
    head = position % ROW
    own_taps = lax.dynamic_slice_in_dim(mr_filter, head * HD, HD, 1)
    mixed_grad_head = head_anti(packed, head_edge, own_taps)

    shared = (widths, packed, kvh, starts, qk)
    attn_head, mixed_head, top, inv = attention_fwd(*shared)
    attn_out = swap(attn_head)
    mixed_before = shift(mixed_head[ROW - 1, TOK - TAPS :], ROW)
    joined, dkv_hi, dkvh = attention_bwd(
        *shared, mixed_grad_head, attn_head, top, inv
    )
    back = shift(dkvh, -ROW)
    filter_part = head_corr(mixed_head, mixed_before, packed)
    mixed, branch_grad = finish(attn_out, key_branch, mixed_grad)
    mixed_edge = shift(mixed[TOK - TAPS :], 1)
    key_grad, value_grad, query_grad = unpack(swap(join(joined, dkv_hi, back)))
    gate_grad = []
    for piece in range(PIECES):
        gate_grad = [
            causal_piece(piece, mixed, mixed_edge, mr_filter, out_grad, gate_grad)
        ]
    gate_grad = gate_grad[0]

    def partner(x, axis, hop):
        pairs = [(i, i ^ hop) for i in range(lax.axis_size(axis))]
        return lax.ppermute(x, axis, pairs)

    rings_n = n_seq // ROW
    tap_share = TAPS // ROW
    own_filter = lax.dynamic_slice_in_dim(mr_filter, head * tap_share, tap_share, 0)
    filter_grad = filter_part + partner(filter_part, "seq", ROW)
    other = partner(filter_grad, "seq", 2 * ROW)
    filter_grad, norms = norm_parts(filter_grad, other, own_filter)
    hop = 1
    while hop < lax.axis_size("ch"):
        norms = norms + partner(norms, "ch", hop)
        hop *= 2
    tap_rows = TAPS // n_seq
    ring_taps = lax.dynamic_slice_in_dim(
        filter_grad, (position // ROW) * (TAPS // rings_n), TAPS // rings_n, 0
    ).reshape(ROW, tap_rows, HD)
    spread_norms = jnp.broadcast_to(norms[None, :tap_rows], (ROW, tap_rows, HD))
    got = swap(jnp.concatenate([ring_taps, spread_norms], 1))
    filter_step = scaled_step(got, tap_rows)
    return (query_grad, key_grad, value_grad, gate_grad, branch_grad, filter_step)


def solution(mesh):
    rows = P("seq", "ch")
    return jax.shard_map(
        per_device,
        mesh=mesh,
        in_specs=(rows, rows, rows, rows, rows, P(None, "ch"), rows, P()),
        out_specs=(rows,) * 6,
        check_vma=False,
    )
```

```python
import jax
import jax.numpy as jnp
from jax import lax
from jax.experimental import pallas as pl
from jax.experimental.pallas import tpu as pltpu
from jax.sharding import PartitionSpec as P


HD = 128
TAPS = 128
SPAN = 4
ROW = 8
DOCS = 64
TOK = 256
EXT = TOK + TAPS
NEG = -1e30
GRANT = pltpu.CompilerParams(vmem_limit_bytes=8 << 20)
STEP = 4
SCALE = HD ** (-0.5)
PIECES = 2


def hbm(*arrays):
    return [pltpu.with_memory_space_constraint(x, pltpu.HBM) for x in arrays]


def pack_kernel(*refs):
    *in_refs, out_ref = refs
    for head in range(out_ref.shape[0]):
        for n, in_ref in enumerate(in_refs):
            out_ref[head, n * TOK : (n + 1) * TOK] = in_ref[:, head * HD : (head + 1) * HD]


def pack(*arrays):
    heads = arrays[0].shape[1] // HD
    n = len(arrays)
    return pl.pallas_call(
        pack_kernel,
        grid=(heads // STEP,),
        in_specs=[pl.BlockSpec((TOK, STEP * HD), lambda h: (0, h))] * n,
        out_specs=pl.BlockSpec((STEP, n * TOK, HD), lambda h: (h, 0, 0)),
        out_shape=pltpu.HBM((heads, n * TOK, HD), arrays[0].dtype),
        compiler_params=GRANT,
        name="pack",
    )(*arrays)


def unpack_kernel(x_ref, *out_refs):
    for head in range(x_ref.shape[0]):
        for n, out_ref in enumerate(out_refs):
            out_ref[:, head * HD : (head + 1) * HD] = x_ref[head, n * TOK : (n + 1) * TOK]


def unpack(x):
    heads, rows, _ = x.shape
    n = rows // TOK
    return pl.pallas_call(
        unpack_kernel,
        grid=(heads // STEP,),
        in_specs=[pl.BlockSpec((STEP, rows, HD), lambda h: (h, 0, 0))],
        out_specs=[pl.BlockSpec((TOK, STEP * HD), lambda h: (0, h))] * n,
        out_shape=[jax.ShapeDtypeStruct((TOK, heads * HD), x.dtype)] * n,
        compiler_params=GRANT,
        name="unpack",
    )(x)


def finish_kernel(x_ref, key_ref, mixed_grad_ref, mixed_ref, branch_ref):
    for head in range(x_ref.shape[0]):
        lanes = slice(head * HD, (head + 1) * HD)
        attn_out = x_ref[head].astype(jnp.float32)
        mixed_ref[:, lanes] = (key_ref[:, lanes].astype(jnp.float32) * attn_out).astype(
            jnp.bfloat16
        )
        branch_ref[:, lanes] = (mixed_grad_ref[:, lanes] * attn_out).astype(jnp.bfloat16)


def finish(attn_out, key, mixed_grad):
    heads = attn_out.shape[0]
    column = pl.BlockSpec((TOK, STEP * HD), lambda h: (0, h))
    shape = pltpu.HBM((TOK, heads * HD), jnp.bfloat16)
    return pl.pallas_call(
        finish_kernel,
        grid=(heads // STEP,),
        in_specs=[pl.BlockSpec((STEP, TOK, HD), lambda h: (h, 0, 0)), column, column],
        out_specs=[column] * 2,
        out_shape=[shape] * 2,
        compiler_params=GRANT,
        name="finish",
    )(attn_out, *hbm(key, mixed_grad))


def join_kernel(joined_ref, own_ref, back_ref, out_ref):
    out_ref[...] = (own_ref[...] + back_ref[...].astype(jnp.float32)).astype(jnp.bfloat16)


def join(joined, own, back):
    part = pl.BlockSpec((2, 2 * TOK, HD), lambda b: (b, 0, 0))
    first = (ROW - SPAN) // 2
    return pl.pallas_call(
        join_kernel,
        grid=(SPAN // 2,),
        in_specs=[pl.BlockSpec(memory_space=pl.ANY), part, part],
        out_specs=pl.BlockSpec((2, 2 * TOK, HD), lambda b: (b + first, 0, 0)),
        out_shape=pltpu.HBM(joined.shape, joined.dtype),
        input_output_aliases={0: 0},
        compiler_params=GRANT,
        name="join",
    )(*hbm(joined), own, back)


def spread(tile_refs, ext_s, sh_s):
    at = 0
    for piece in tile_refs:
        ext_s[at : at + piece.shape[0]] = piece.astype(jnp.float32)
        at += piece.shape[0]
    ext_s[at:] = jnp.zeros((8, HD), jnp.float32)
    for r in range(8):
        sh_s[r] = ext_s[pl.ds(r, EXT)]


HALF = TOK // 2


def ahead(k, r):
    return r, k * 8


def behind(k, r):
    return ((8 - r) % 8, TAPS - 8 - k * 8) if r else (0, TAPS - k * 8)


def filtered(sh_s, w_s, where, half):
    def group(k, total):
        taps = w_s[pl.ds(pl.multiple_of(k * 8, 8), 8)]
        for r in range(8):
            slot, start = where(k, r)
            start = pl.multiple_of(start + half * HALF, 8)
            total = total + taps[r : r + 1] * sh_s[slot, pl.ds(start, HALF)]
        return total

    return lax.fori_loop(0, TAPS // 8, group, jnp.zeros((HALF, HD), jnp.float32))


def anti_kernel(g_ref, edge_ref, w_ref, out_ref, ext_s, sh_s, w_s):
    spread((g_ref[...], edge_ref[...]), ext_s, sh_s)
    w_s[...] = w_ref[...].astype(jnp.float32)
    for half in range(2):
        out_ref[half * HALF : (half + 1) * HALF] = filtered(sh_s, w_s, ahead, half)


def anti(conv_grad, edge, weights):
    column = lambda rows: pl.BlockSpec((rows, HD), lambda c: (0, c))
    return pl.pallas_call(
        anti_kernel,
        grid=(conv_grad.shape[1] // HD,),
        in_specs=[column(TOK), column(TAPS), column(TAPS)],
        out_specs=column(TOK),
        out_shape=pltpu.HBM(conv_grad.shape, jnp.float32),
        scratch_shapes=[
            pltpu.VMEM((EXT + 8, HD), jnp.float32),
            pltpu.VMEM((8, EXT, HD), jnp.float32),
            pltpu.VMEM((TAPS, HD), jnp.float32),
        ],
        compiler_params=GRANT,
        name="anti",
    )(conv_grad, edge, weights)


def causal_kernel(m_ref, edge_ref, w_ref, grad_ref, *refs):
    out_ref, ext_s, sh_s, w_s = refs[-4:]
    spread((edge_ref[...], m_ref[...]), ext_s, sh_s)
    w_s[...] = w_ref[...].astype(jnp.float32)
    for half in range(2):
        rows = slice(half * HALF, (half + 1) * HALF)
        conv_out = filtered(sh_s, w_s, behind, half)
        out_ref[rows] = (grad_ref[rows].astype(jnp.float32) * conv_out).astype(jnp.bfloat16)


def causal_piece(piece, mixed, edge, weights, out_grad, before):
    tiles = mixed.shape[1] // HD // PIECES
    column = lambda rows: pl.BlockSpec((rows, HD), lambda c: (0, c + piece * tiles))
    return pl.pallas_call(
        causal_kernel,
        grid=(tiles,),
        in_specs=[column(TOK), column(TAPS), column(TAPS), column(TOK)]
        + [pl.BlockSpec(memory_space=pl.ANY)] * len(before),
        out_specs=column(TOK),
        out_shape=pltpu.HBM(mixed.shape, jnp.bfloat16),
        scratch_shapes=[
            pltpu.VMEM((EXT + 8, HD), jnp.float32),
            pltpu.VMEM((8, EXT, HD), jnp.float32),
            pltpu.VMEM((TAPS, HD), jnp.float32),
        ],
        input_output_aliases={4: 0} if before else {},
        compiler_params=GRANT,
        name="causal",
    )(*hbm(mixed, edge, weights, out_grad, *before))


def head_anti_kernel(cur_ref, next_ref, edge_ref, w_ref, out_ref, ext_s, sh_s, w_s):
    last = pl.program_id(0) == ROW - 1
    after = jnp.where(last, edge_ref[...].astype(jnp.float32), next_ref[0].astype(jnp.float32))
    spread((cur_ref[0], after), ext_s, sh_s)
    w_s[...] = w_ref[...].astype(jnp.float32)
    for half in range(2):
        out_ref[0, half * HALF : (half + 1) * HALF] = filtered(sh_s, w_s, ahead, half)


def head_anti(packed, edge, weights):
    return pl.pallas_call(
        head_anti_kernel,
        grid=(ROW,),
        in_specs=[
            pl.BlockSpec((1, TOK, HD), lambda b: (b, 0, 0)),
            pl.BlockSpec((1, TAPS, HD), lambda b: (jnp.minimum(b + 1, ROW - 1), 0, 0)),
            pl.BlockSpec((TAPS, HD), lambda b: (0, 0)),
            pl.BlockSpec((TAPS, HD), lambda b: (0, 0)),
        ],
        out_specs=pl.BlockSpec((1, TOK, HD), lambda b: (b, 0, 0)),
        out_shape=pltpu.HBM((ROW, TOK, HD), jnp.float32),
        scratch_shapes=[
            pltpu.VMEM((EXT + 8, HD), jnp.float32),
            pltpu.VMEM((8, EXT, HD), jnp.float32),
            pltpu.VMEM((TAPS, HD), jnp.float32),
        ],
        compiler_params=GRANT,
        name="head_anti",
    )(packed, packed, edge, weights)


def head_corr_kernel(cur_ref, prev_ref, edge_ref, g_ref, out_ref, ext_s, sh_s, g_s, part_s):
    block = pl.program_id(0)
    before = jnp.where(
        block == 0, edge_ref[...].astype(jnp.float32), prev_ref[0].astype(jnp.float32)
    )
    spread((before, cur_ref[0]), ext_s, sh_s)
    g_s[...] = g_ref[0].astype(jnp.float32)

    @pl.when(block == 0)
    def _():
        part_s[...] = jnp.zeros_like(part_s)

    rows = TOK // 2

    def half_of(half, _):
        base = pl.multiple_of(half * rows, rows)
        g = [g_s[pl.ds(base + 8 * i, 8)] for i in range(rows // 8)]
        for r in range(8):
            for group in range(2):
                low = (72 if r == 0 else 64) - 64 * group
                piece = [
                    sh_s[(8 - r) % 8, pl.ds(base + low + 8 * i, 8)] for i in range(rows // 8 + 7)
                ]
                for kk in range(8):
                    total = g[0] * piece[7 - kk]
                    for i in range(1, rows // 8):
                        total = total + g[i] * piece[i + 7 - kk]
                    part_s[r, 8 * group + kk] += total
        return 0

    lax.fori_loop(0, 2, half_of, 0)

    @pl.when(block == ROW - 1)
    def _():
        for r in range(8):
            out_ref[pl.ds(r, TAPS // 8, stride=8)] = jnp.sum(part_s[r], 1)


def head_corr(mixed, edge, packed):
    return pl.pallas_call(
        head_corr_kernel,
        grid=(ROW,),
        in_specs=[
            pl.BlockSpec((1, TOK, HD), lambda b: (b, 0, 0)),
            pl.BlockSpec((1, TAPS, HD), lambda b: (jnp.maximum(b - 1, 0), 1, 0)),
            pl.BlockSpec((TAPS, HD), lambda b: (0, 0)),
            pl.BlockSpec((1, TOK, HD), lambda b: (b, 0, 0)),
        ],
        out_specs=pl.BlockSpec((TAPS, HD), lambda b: (0, 0)),
        out_shape=jax.ShapeDtypeStruct((TAPS, HD), jnp.float32),
        scratch_shapes=[
            pltpu.VMEM((EXT + 8, HD), jnp.float32),
            pltpu.VMEM((8, EXT, HD), jnp.float32),
            pltpu.VMEM((TOK, HD), jnp.float32),
            pltpu.VMEM((8, TAPS // 8, 8, HD), jnp.float32),
        ],
        compiler_params=GRANT,
        name="head_corr",
    )(mixed, mixed, edge, packed)


def dot_nn(a, b):
    return jnp.dot(a, b, preferred_element_type=jnp.float32)


def norm_kernel(a_ref, b_ref, w_ref, sum_ref, norms_ref):
    total = a_ref[...] + b_ref[...]
    sum_ref[...] = total
    filter_sq = jnp.sum(jnp.square(w_ref[...].astype(jnp.float32)))
    norms_ref[...] = jnp.zeros_like(norms_ref)
    norms_ref[0:1] = jnp.full((1, HD), filter_sq, jnp.float32)
    norms_ref[1:2] = jnp.full((1, HD), jnp.sum(total * total), jnp.float32)


def norm_parts(a, b, weights):
    return pl.pallas_call(
        norm_kernel,
        out_shape=[
            jax.ShapeDtypeStruct(a.shape, jnp.float32),
            jax.ShapeDtypeStruct((8, HD), jnp.float32),
        ],
        compiler_params=GRANT,
        name="norm_parts",
    )(a, b, weights)


def step_kernel(got_ref, out_ref):
    rows = out_ref.shape[0]
    norms = jnp.sum(got_ref[:, rows : rows + 2], 0)
    trust = jnp.sqrt(norms[0:1]) / jnp.sqrt(norms[1:2] + 1e-06)
    for head in range(ROW):
        out_ref[:, head * HD : (head + 1) * HD] = trust * got_ref[head, :rows]


def scaled_step(got, rows):
    return pl.pallas_call(
        step_kernel,
        out_shape=jax.ShapeDtypeStruct((rows, ROW * HD), jnp.float32),
        compiler_params=GRANT,
        name="scaled_step",
    )(got)


def window_of(block, width):
    first = block + (SPAN + 1 - width)
    return first, pl.ds(pl.multiple_of(first * TOK, TOK), width * TOK)


def key_blocks(packed_ref, kvh_ref):
    for b in range(SPAN + ROW):
        src = kvh_ref if b < SPAN else packed_ref
        at = b if b < SPAN else b - SPAN
        skip = 0 if b < SPAN else TOK
        k = src[at, skip : skip + TOK]
        yield b, slice(b * TOK, (b + 1) * TOK), k, src[at, skip + TOK :]


def masked_scores(k, q, starts, first, width):
    scores = dot_nn(k, q.T)
    key_at = lax.broadcasted_iota(jnp.int32, scores.shape, 0)
    allowed = key_at >= starts - first * TOK
    own = (width - 1) * TOK
    query_at = lax.broadcasted_iota(jnp.int32, (TOK, TOK), 1)
    causal = allowed[own:] & (lax.broadcasted_iota(jnp.int32, (TOK, TOK), 0) <= query_at)
    diagonal = jnp.where(causal, scores[own:], NEG)
    if width == 1:
        return diagonal
    return jnp.concatenate([jnp.where(allowed[:own], scores[:own], NEG), diagonal], 0)


def each_block(width_ref, attend):
    def step(block, carry):
        for width in range(1, SPAN + 2):
            pl.when(width_ref[block] == width)(lambda width=width: attend(block, width))
        return carry

    lax.fori_loop(0, ROW, step, 0)


def fwd_kernel(
    width_ref, packed_ref, kvh_ref, starts_ref, qk_ref,
    out_ref, mixed_ref, top_ref, inv_ref, k_s, vt_s,
):
    for b, rows, k, v in key_blocks(packed_ref, kvh_ref):
        k_s[rows] = k
        vt_s[b] = v.T

    def attend(block, width):
        first, rows = window_of(block, width)
        q = qk_ref[block, :TOK]
        vt = jnp.concatenate([vt_s[first + n] for n in range(width)], 1)
        scores = masked_scores(k_s[rows], q, starts_ref[block], first, width)
        top = jnp.max(scores, 0, keepdims=True)
        weights = jnp.exp((scores - top) * SCALE)
        inv = 1.0 / jnp.sum(weights, 0, keepdims=True)
        top_ref[block] = top
        inv_ref[block] = inv
        probs = (weights * inv).astype(jnp.bfloat16)
        out = dot_nn(vt, probs).astype(jnp.bfloat16).T
        out_ref[block] = out
        key = qk_ref[block, TOK:].astype(jnp.float32)
        mixed_ref[block] = (key * out.astype(jnp.float32)).astype(jnp.bfloat16)

    each_block(width_ref, attend)


def bwd_kernel(
    width_ref, packed_ref, kvh_ref, starts_ref, qk_ref, mixed_grad_ref,
    out_ref, top_ref, inv_ref,
    joined_ref, dkv_hi_ref, dkvh_ref, k_s, v_s, kt_s, dk_s, dv_s,
):
    for b, rows, k, v in key_blocks(packed_ref, kvh_ref):
        k_s[rows] = k
        v_s[rows] = v
        kt_s[b] = k.T
    dk_s[...] = jnp.zeros_like(dk_s)
    dv_s[...] = jnp.zeros_like(dv_s)

    def attend(block, width):
        first, rows = window_of(block, width)
        q = qk_ref[block, :TOK]
        key = qk_ref[block, TOK:].astype(jnp.float32)
        grad = (mixed_grad_ref[block] * key).astype(jnp.bfloat16)
        grad_t = grad.T
        kt = jnp.concatenate([kt_s[first + n] for n in range(width)], 1)
        scores = masked_scores(k_s[rows], q, starts_ref[block], first, width)
        weights = jnp.exp((scores - top_ref[block]) * SCALE) * inv_ref[block]
        probs = weights.astype(jnp.bfloat16)
        row_dot = jnp.sum(
            out_ref[block].T.astype(jnp.float32) * grad_t.astype(jnp.float32), 0, keepdims=True
        )
        prob_grad = dot_nn(v_s[rows], grad_t)
        score_grad = (weights * (prob_grad - row_dot)).astype(jnp.bfloat16)
        dq = (dot_nn(kt, score_grad) * SCALE).astype(jnp.bfloat16).T
        joined_ref[block, 2 * TOK :] = dq
        dk_s[rows] += dot_nn(score_grad, q)
        dv_s[rows] += dot_nn(probs, grad)

    each_block(width_ref, attend)
    outs = (dkvh_ref, joined_ref, dkv_hi_ref)
    for b in range(SPAN + ROW):
        rows = slice(b * TOK, (b + 1) * TOK)
        ref = outs[b // SPAN]
        ref[b % SPAN, :TOK] = (dk_s[rows] * SCALE).astype(ref.dtype)
        ref[b % SPAN, TOK : 2 * TOK] = dv_s[rows].astype(ref.dtype)


KEYS = (SPAN + ROW) * TOK


def whole(*shape):
    return pl.BlockSpec(shape, lambda b, w: (0,) * len(shape))


VMEM = pl.BlockSpec(memory_space=pltpu.VMEM)


def attention_fwd(widths, packed, kvh, starts, qk):
    operands = [packed, *hbm(kvh), starts, qk]
    return pl.pallas_call(
        fwd_kernel,
        grid_spec=pltpu.PrefetchScalarGridSpec(
            num_scalar_prefetch=1,
            grid=(1,),
            in_specs=[VMEM, whole(SPAN, 2 * TOK, HD), VMEM, VMEM],
            out_specs=[whole(ROW, TOK, HD), VMEM, VMEM, VMEM],
            scratch_shapes=[
                pltpu.VMEM((KEYS, HD), jnp.bfloat16),
                pltpu.VMEM((SPAN + ROW, HD, TOK), jnp.bfloat16),
            ],
        ),
        out_shape=[
            pltpu.HBM((ROW, TOK, HD), jnp.bfloat16),
            jax.ShapeDtypeStruct((ROW, TOK, HD), jnp.bfloat16),
            jax.ShapeDtypeStruct((ROW, 1, TOK), jnp.float32),
            jax.ShapeDtypeStruct((ROW, 1, TOK), jnp.float32),
        ],
        compiler_params=pltpu.CompilerParams(vmem_limit_bytes=20 << 20),
        name="attn_fwd",
    )(widths, *operands)


def attention_bwd(widths, packed, kvh, starts, qk, mixed_grad, out, top, inv):
    operands = [packed, *hbm(kvh), starts, qk, *hbm(mixed_grad, out), top, inv]
    return pl.pallas_call(
        bwd_kernel,
        grid_spec=pltpu.PrefetchScalarGridSpec(
            num_scalar_prefetch=1,
            grid=(1,),
            in_specs=[VMEM, whole(SPAN, 2 * TOK, HD), VMEM, VMEM]
            + [whole(ROW, TOK, HD)] * 2
            + [VMEM] * 2,
            out_specs=[whole(ROW, 3 * TOK, HD), VMEM, VMEM],
            scratch_shapes=[
                pltpu.VMEM((KEYS, HD), jnp.bfloat16),
                pltpu.VMEM((KEYS, HD), jnp.bfloat16),
                pltpu.VMEM((SPAN + ROW, HD, TOK), jnp.bfloat16),
                pltpu.VMEM((KEYS, HD), jnp.float32),
                pltpu.VMEM((KEYS, HD), jnp.float32),
            ],
        ),
        out_shape=[
            pltpu.HBM((ROW, 3 * TOK, HD), jnp.bfloat16),
            jax.ShapeDtypeStruct((SPAN, 2 * TOK, HD), jnp.float32),
            jax.ShapeDtypeStruct((SPAN, 2 * TOK, HD), jnp.bfloat16),
        ],
        compiler_params=pltpu.CompilerParams(vmem_limit_bytes=28 << 20),
        name="attn_bwd",
    )(widths, *operands)


def per_device(
    queries_in, keys_in, values_in, gate_branch, key_branch, mr_filter, out_grad, doc_ids
):
    n_seq = lax.axis_size("seq")
    position = lax.axis_index("seq")
    rings = [list(range(g, g + ROW)) for g in range(0, n_seq, ROW)]

    def swap(x, groups=rings, axis="seq"):
        return lax.all_to_all(x, axis, 0, 0, axis_index_groups=groups, tiled=True)

    def shift(x, by):
        pairs = [(i, i + by) for i in range(n_seq) if 0 <= i + by < n_seq]
        return lax.ppermute(x, "seq", pairs)

    doc_front = jnp.concatenate([jnp.full((SPAN * TOK,), -1, jnp.int32), doc_ids], 0)
    docs = lax.dynamic_slice_in_dim(
        doc_front, (position // ROW) * (ROW * TOK), (SPAN + ROW) * TOK, 0
    ).reshape(SPAN + ROW, TOK)
    widths = jnp.ones((ROW,), jnp.int32)
    for back in range(1, SPAN + 1):
        widths = widths + (docs[SPAN - back : SPAN + ROW - back, -1] == docs[SPAN:, 0])
    numbers = jnp.arange(DOCS, dtype=jnp.int32)[:, None]
    first_rows = jnp.sum((doc_ids[None] < numbers).astype(jnp.int32), 1, keepdims=True)
    first_rows = first_rows - ((position // ROW) * ROW - SPAN) * TOK
    starts = jnp.sum(jnp.where(docs[SPAN:].reshape(1, -1) == numbers, first_rows, 0), 0)
    starts = starts.reshape(ROW, 1, TOK)

    conv_grad = (out_grad.astype(jnp.float32) * gate_branch.astype(jnp.float32)).astype(
        jnp.bfloat16
    )
    grad_edge = shift(conv_grad[:TAPS], -1)
    packed = swap(pack(conv_grad, keys_in, values_in))
    mixed_grad = anti(conv_grad, grad_edge, mr_filter)
    qk = swap(pack(queries_in, key_branch))

    kvh = shift(packed[ROW - SPAN :, TOK:], ROW)
    head_edge = shift(packed[0, :TAPS], -ROW)
    head = position % ROW
    own_taps = lax.dynamic_slice_in_dim(mr_filter, head * HD, HD, 1)
    mixed_grad_head = head_anti(packed, head_edge, own_taps)

    shared = (widths, packed, kvh, starts, qk)
    attn_head, mixed_head, top, inv = attention_fwd(*shared)
    attn_out = swap(attn_head)
    mixed_before = shift(mixed_head[ROW - 1, TOK - TAPS :], ROW)
    joined, dkv_hi, dkvh = attention_bwd(
        *shared, mixed_grad_head, attn_head, top, inv
    )
    back = shift(dkvh, -ROW)
    filter_part = head_corr(mixed_head, mixed_before, packed)
    mixed, branch_grad = finish(attn_out, key_branch, mixed_grad)
    mixed_edge = shift(mixed[TOK - TAPS :], 1)
    key_grad, value_grad, query_grad = unpack(swap(join(joined, dkv_hi, back)))
    gate_grad = []
    for piece in range(PIECES):
        gate_grad = [
            causal_piece(piece, mixed, mixed_edge, mr_filter, out_grad, gate_grad)
        ]
    gate_grad = gate_grad[0]

    def partner(x, axis, hop):
        pairs = [(i, i ^ hop) for i in range(lax.axis_size(axis))]
        return lax.ppermute(x, axis, pairs)

    rings_n = n_seq // ROW
    tap_share = TAPS // ROW
    own_filter = lax.dynamic_slice_in_dim(mr_filter, head * tap_share, tap_share, 0)
    filter_grad = filter_part + partner(filter_part, "seq", ROW)
    other = partner(filter_grad, "seq", 2 * ROW)
    filter_grad, norms = norm_parts(filter_grad, other, own_filter)
    hop = 1
    while hop < lax.axis_size("ch"):
        norms = norms + partner(norms, "ch", hop)
        hop *= 2
    tap_rows = TAPS // n_seq
    ring_taps = lax.dynamic_slice_in_dim(
        filter_grad, (position // ROW) * (TAPS // rings_n), TAPS // rings_n, 0
    ).reshape(ROW, tap_rows, HD)
    spread_norms = jnp.broadcast_to(norms[None, :tap_rows], (ROW, tap_rows, HD))
    got = swap(jnp.concatenate([ring_taps, spread_norms], 1))
    filter_step = scaled_step(got, tap_rows)
    return (query_grad, key_grad, value_grad, gate_grad, branch_grad, filter_step)


def solution(mesh):
    rows = P("seq", "ch")
    return jax.shard_map(
        per_device,
        mesh=mesh,
        in_specs=(rows, rows, rows, rows, rows, P(None, "ch"), rows, P()),
        out_specs=(rows,) * 6,
        check_vma=False,
    )
```

```python
import jax
import jax.numpy as jnp
from jax import lax
from jax.experimental import pallas as pl
from jax.experimental.pallas import tpu as pltpu
from jax.sharding import PartitionSpec as P


HD = 128
TAPS = 128
SPAN = 4
ROW = 8
DOCS = 64
TOK = 256
EXT = TOK + TAPS
NEG = -1e30
GRANT = pltpu.CompilerParams(vmem_limit_bytes=8 << 20)
STEP = 4
SCALE = HD ** (-0.5)
PIECES = 4


def hbm(*arrays):
    return [pltpu.with_memory_space_constraint(x, pltpu.HBM) for x in arrays]


def pack_kernel(*refs):
    *in_refs, out_ref = refs
    for head in range(out_ref.shape[0]):
        for n, in_ref in enumerate(in_refs):
            out_ref[head, n * TOK : (n + 1) * TOK] = in_ref[:, head * HD : (head + 1) * HD]


def pack(*arrays):
    heads = arrays[0].shape[1] // HD
    n = len(arrays)
    return pl.pallas_call(
        pack_kernel,
        grid=(heads // STEP,),
        in_specs=[pl.BlockSpec((TOK, STEP * HD), lambda h: (0, h))] * n,
        out_specs=pl.BlockSpec((STEP, n * TOK, HD), lambda h: (h, 0, 0)),
        out_shape=pltpu.HBM((heads, n * TOK, HD), arrays[0].dtype),
        compiler_params=GRANT,
        name="pack",
    )(*arrays)


def unpack_kernel(x_ref, *out_refs):
    for head in range(x_ref.shape[0]):
        for n, out_ref in enumerate(out_refs):
            out_ref[:, head * HD : (head + 1) * HD] = x_ref[head, n * TOK : (n + 1) * TOK]


def unpack(x):
    heads, rows, _ = x.shape
    n = rows // TOK
    return pl.pallas_call(
        unpack_kernel,
        grid=(heads // STEP,),
        in_specs=[pl.BlockSpec((STEP, rows, HD), lambda h: (h, 0, 0))],
        out_specs=[pl.BlockSpec((TOK, STEP * HD), lambda h: (0, h))] * n,
        out_shape=[jax.ShapeDtypeStruct((TOK, heads * HD), x.dtype)] * n,
        compiler_params=GRANT,
        name="unpack",
    )(x)


def finish_kernel(x_ref, key_ref, mixed_grad_ref, mixed_ref, branch_ref, edge_ref):
    for head in range(x_ref.shape[0]):
        lanes = slice(head * HD, (head + 1) * HD)
        attn_out = x_ref[head].astype(jnp.float32)
        mixed_ref[:, lanes] = (key_ref[:, lanes].astype(jnp.float32) * attn_out).astype(
            jnp.bfloat16
        )
        branch_ref[:, lanes] = (mixed_grad_ref[:, lanes] * attn_out).astype(jnp.bfloat16)
    edge_ref[...] = mixed_ref[TOK - TAPS :]


def finish(attn_out, key, mixed_grad):
    heads = attn_out.shape[0]
    column = pl.BlockSpec((TOK, STEP * HD), lambda h: (0, h))
    shape = pltpu.HBM((TOK, heads * HD), jnp.bfloat16)
    return pl.pallas_call(
        finish_kernel,
        grid=(heads // STEP,),
        in_specs=[pl.BlockSpec((STEP, TOK, HD), lambda h: (h, 0, 0)), column, column],
        out_specs=[column] * 2 + [pl.BlockSpec((TAPS, STEP * HD), lambda h: (0, h))],
        out_shape=[shape] * 2 + [jax.ShapeDtypeStruct((TAPS, heads * HD), jnp.bfloat16)],
        compiler_params=GRANT,
        name="finish",
    )(attn_out, *hbm(key, mixed_grad))


def join_kernel(joined_ref, own_ref, back_ref, out_ref):
    out_ref[...] = (own_ref[...] + back_ref[...].astype(jnp.float32)).astype(jnp.bfloat16)


def join(joined, own, back):
    part = pl.BlockSpec((2, 2 * TOK, HD), lambda b: (b, 0, 0))
    first = (ROW - SPAN) // 2
    return pl.pallas_call(
        join_kernel,
        grid=(SPAN // 2,),
        in_specs=[pl.BlockSpec(memory_space=pl.ANY), part, part],
        out_specs=pl.BlockSpec((2, 2 * TOK, HD), lambda b: (b + first, 0, 0)),
        out_shape=pltpu.HBM(joined.shape, joined.dtype),
        input_output_aliases={0: 0},
        compiler_params=GRANT,
        name="join",
    )(*hbm(joined), own, back)


def spread(tile_refs, ext_s, sh_s):
    at = 0
    for piece in tile_refs:
        ext_s[at : at + piece.shape[0]] = piece.astype(jnp.float32)
        at += piece.shape[0]
    ext_s[at:] = jnp.zeros((8, HD), jnp.float32)
    for r in range(8):
        sh_s[r] = ext_s[pl.ds(r, EXT)]


HALF = TOK // 2


def ahead(k, r):
    return r, k * 8


def behind(k, r):
    return ((8 - r) % 8, TAPS - 8 - k * 8) if r else (0, TAPS - k * 8)


def filtered(sh_s, w_s, where, half):
    def group(k, total):
        taps = w_s[pl.ds(pl.multiple_of(k * 8, 8), 8)]
        for r in range(8):
            slot, start = where(k, r)
            start = pl.multiple_of(start + half * HALF, 8)
            total = total + taps[r : r + 1] * sh_s[slot, pl.ds(start, HALF)]
        return total

    return lax.fori_loop(0, TAPS // 8, group, jnp.zeros((HALF, HD), jnp.float32))


def anti_kernel(g_ref, edge_ref, w_ref, out_ref, ext_s, sh_s, w_s):
    spread((g_ref[...], edge_ref[...]), ext_s, sh_s)
    w_s[...] = w_ref[...].astype(jnp.float32)
    for half in range(2):
        out_ref[half * HALF : (half + 1) * HALF] = filtered(sh_s, w_s, ahead, half)


def anti(conv_grad, edge, weights):
    column = lambda rows: pl.BlockSpec((rows, HD), lambda c: (0, c))
    return pl.pallas_call(
        anti_kernel,
        grid=(conv_grad.shape[1] // HD,),
        in_specs=[column(TOK), column(TAPS), column(TAPS)],
        out_specs=column(TOK),
        out_shape=pltpu.HBM(conv_grad.shape, jnp.float32),
        scratch_shapes=[
            pltpu.VMEM((EXT + 8, HD), jnp.float32),
            pltpu.VMEM((8, EXT, HD), jnp.float32),
            pltpu.VMEM((TAPS, HD), jnp.float32),
        ],
        compiler_params=GRANT,
        name="anti",
    )(conv_grad, edge, weights)


def causal_kernel(m_ref, edge_ref, w_ref, grad_ref, *refs):
    out_ref, ext_s, sh_s, w_s = refs[-4:]
    spread((edge_ref[...], m_ref[...]), ext_s, sh_s)
    w_s[...] = w_ref[...].astype(jnp.float32)
    for half in range(2):
        rows = slice(half * HALF, (half + 1) * HALF)
        conv_out = filtered(sh_s, w_s, behind, half)
        out_ref[rows] = (grad_ref[rows].astype(jnp.float32) * conv_out).astype(jnp.bfloat16)


def causal_piece(piece, mixed, edge, weights, out_grad, before):
    tiles = mixed.shape[1] // HD // PIECES
    column = lambda rows: pl.BlockSpec((rows, HD), lambda c: (0, c + piece * tiles))
    return pl.pallas_call(
        causal_kernel,
        grid=(tiles,),
        in_specs=[column(TOK), column(TAPS), column(TAPS), column(TOK)]
        + [pl.BlockSpec(memory_space=pl.ANY)] * len(before),
        out_specs=column(TOK),
        out_shape=pltpu.HBM(mixed.shape, jnp.bfloat16),
        scratch_shapes=[
            pltpu.VMEM((EXT + 8, HD), jnp.float32),
            pltpu.VMEM((8, EXT, HD), jnp.float32),
            pltpu.VMEM((TAPS, HD), jnp.float32),
        ],
        input_output_aliases={4: 0} if before else {},
        compiler_params=GRANT,
        name="causal",
    )(*hbm(mixed, edge, weights, out_grad, *before))


def head_anti_kernel(cur_ref, next_ref, edge_ref, w_ref, out_ref, ext_s, sh_s, w_s):
    last = pl.program_id(0) == ROW - 1
    after = jnp.where(last, edge_ref[...].astype(jnp.float32), next_ref[0].astype(jnp.float32))
    spread((cur_ref[0], after), ext_s, sh_s)
    w_s[...] = w_ref[...].astype(jnp.float32)
    for half in range(2):
        out_ref[0, half * HALF : (half + 1) * HALF] = filtered(sh_s, w_s, ahead, half)


def head_anti(packed, edge, weights):
    return pl.pallas_call(
        head_anti_kernel,
        grid=(ROW,),
        in_specs=[
            pl.BlockSpec((1, TOK, HD), lambda b: (b, 0, 0)),
            pl.BlockSpec((1, TAPS, HD), lambda b: (jnp.minimum(b + 1, ROW - 1), 0, 0)),
            pl.BlockSpec((TAPS, HD), lambda b: (0, 0)),
            pl.BlockSpec((TAPS, HD), lambda b: (0, 0)),
        ],
        out_specs=pl.BlockSpec((1, TOK, HD), lambda b: (b, 0, 0)),
        out_shape=pltpu.HBM((ROW, TOK, HD), jnp.float32),
        scratch_shapes=[
            pltpu.VMEM((EXT + 8, HD), jnp.float32),
            pltpu.VMEM((8, EXT, HD), jnp.float32),
            pltpu.VMEM((TAPS, HD), jnp.float32),
        ],
        compiler_params=GRANT,
        name="head_anti",
    )(packed, packed, edge, weights)


def head_corr_kernel(cur_ref, prev_ref, edge_ref, g_ref, out_ref, ext_s, sh_s, g_s, part_s):
    block = pl.program_id(0)
    before = jnp.where(
        block == 0, edge_ref[...].astype(jnp.float32), prev_ref[0].astype(jnp.float32)
    )
    spread((before, cur_ref[0]), ext_s, sh_s)
    g_s[...] = g_ref[0].astype(jnp.float32)

    @pl.when(block == 0)
    def _():
        part_s[...] = jnp.zeros_like(part_s)

    rows = TOK // 2

    def half_of(half, _):
        base = pl.multiple_of(half * rows, rows)
        g = [g_s[pl.ds(base + 8 * i, 8)] for i in range(rows // 8)]
        for r in range(8):
            for group in range(2):
                low = (72 if r == 0 else 64) - 64 * group
                piece = [
                    sh_s[(8 - r) % 8, pl.ds(base + low + 8 * i, 8)] for i in range(rows // 8 + 7)
                ]
                for kk in range(8):
                    total = g[0] * piece[7 - kk]
                    for i in range(1, rows // 8):
                        total = total + g[i] * piece[i + 7 - kk]
                    part_s[r, 8 * group + kk] += total
        return 0

    lax.fori_loop(0, 2, half_of, 0)

    @pl.when(block == ROW - 1)
    def _():
        for r in range(8):
            out_ref[pl.ds(r, TAPS // 8, stride=8)] = jnp.sum(part_s[r], 1)


def head_corr(mixed, edge, packed):
    return pl.pallas_call(
        head_corr_kernel,
        grid=(ROW,),
        in_specs=[
            pl.BlockSpec((1, TOK, HD), lambda b: (b, 0, 0)),
            pl.BlockSpec((1, TAPS, HD), lambda b: (jnp.maximum(b - 1, 0), 1, 0)),
            pl.BlockSpec((TAPS, HD), lambda b: (0, 0)),
            pl.BlockSpec((1, TOK, HD), lambda b: (b, 0, 0)),
        ],
        out_specs=pl.BlockSpec((TAPS, HD), lambda b: (0, 0)),
        out_shape=jax.ShapeDtypeStruct((TAPS, HD), jnp.float32),
        scratch_shapes=[
            pltpu.VMEM((EXT + 8, HD), jnp.float32),
            pltpu.VMEM((8, EXT, HD), jnp.float32),
            pltpu.VMEM((TOK, HD), jnp.float32),
            pltpu.VMEM((8, TAPS // 8, 8, HD), jnp.float32),
        ],
        compiler_params=GRANT,
        name="head_corr",
    )(*hbm(mixed, mixed), edge, packed)


def dot_nn(a, b):
    return jnp.dot(a, b, preferred_element_type=jnp.float32)


def norm_kernel(a_ref, b_ref, w_ref, sum_ref, norms_ref):
    total = a_ref[...] + b_ref[...]
    sum_ref[...] = total
    filter_sq = jnp.sum(jnp.square(w_ref[...].astype(jnp.float32)))
    norms_ref[...] = jnp.zeros_like(norms_ref)
    norms_ref[0:1] = jnp.full((1, HD), filter_sq, jnp.float32)
    norms_ref[1:2] = jnp.full((1, HD), jnp.sum(total * total), jnp.float32)


def norm_parts(a, b, weights):
    return pl.pallas_call(
        norm_kernel,
        out_shape=[
            jax.ShapeDtypeStruct(a.shape, jnp.float32),
            jax.ShapeDtypeStruct((8, HD), jnp.float32),
        ],
        compiler_params=GRANT,
        name="norm_parts",
    )(a, b, weights)


def step_kernel(got_ref, out_ref):
    rows = out_ref.shape[0]
    norms = jnp.sum(got_ref[:, rows : rows + 2], 0)
    trust = jnp.sqrt(norms[0:1]) / jnp.sqrt(norms[1:2] + 1e-06)
    for head in range(ROW):
        out_ref[:, head * HD : (head + 1) * HD] = trust * got_ref[head, :rows]


def scaled_step(got, rows):
    return pl.pallas_call(
        step_kernel,
        out_shape=jax.ShapeDtypeStruct((rows, ROW * HD), jnp.float32),
        compiler_params=GRANT,
        name="scaled_step",
    )(got)


def window_of(block, width):
    first = block + (SPAN + 1 - width)
    return first, pl.ds(pl.multiple_of(first * TOK, TOK), width * TOK)


def key_blocks(packed_ref, kvh_ref):
    for b in range(SPAN + ROW):
        src = kvh_ref if b < SPAN else packed_ref
        at = b if b < SPAN else b - SPAN
        skip = 0 if b < SPAN else TOK
        k = src[at, skip : skip + TOK]
        yield b, slice(b * TOK, (b + 1) * TOK), k, src[at, skip + TOK :]


def masked_scores(k, q, starts, first, width):
    scores = dot_nn(k, q.T)
    key_at = lax.broadcasted_iota(jnp.int32, scores.shape, 0)
    allowed = key_at >= starts - first * TOK
    own = (width - 1) * TOK
    query_at = lax.broadcasted_iota(jnp.int32, (TOK, TOK), 1)
    causal = allowed[own:] & (lax.broadcasted_iota(jnp.int32, (TOK, TOK), 0) <= query_at)
    diagonal = jnp.where(causal, scores[own:], NEG)
    if width == 1:
        return diagonal
    return jnp.concatenate([jnp.where(allowed[:own], scores[:own], NEG), diagonal], 0)


def each_block(width_ref, attend):
    def step(block, carry):
        for width in range(1, SPAN + 2):
            pl.when(width_ref[block] == width)(lambda width=width: attend(block, width))
        return carry

    lax.fori_loop(0, ROW, step, 0)


def fwd_kernel(
    width_ref, packed_ref, kvh_ref, starts_ref, qk_ref,
    out_ref, mixed_ref, top_ref, inv_ref, k_s, vt_s,
):
    for b, rows, k, v in key_blocks(packed_ref, kvh_ref):
        k_s[rows] = k
        vt_s[b] = v.T

    def attend(block, width):
        first, rows = window_of(block, width)
        q = qk_ref[block, :TOK]
        vt = jnp.concatenate([vt_s[first + n] for n in range(width)], 1)
        scores = masked_scores(k_s[rows], q, starts_ref[block], first, width)
        top = jnp.max(scores, 0, keepdims=True)
        weights = jnp.exp((scores - top) * SCALE)
        inv = 1.0 / jnp.sum(weights, 0, keepdims=True)
        top_ref[block] = top
        inv_ref[block] = inv
        probs = (weights * inv).astype(jnp.bfloat16)
        out = dot_nn(vt, probs).astype(jnp.bfloat16).T
        out_ref[block] = out
        key = qk_ref[block, TOK:].astype(jnp.float32)
        mixed_ref[block] = (key * out.astype(jnp.float32)).astype(jnp.bfloat16)

    each_block(width_ref, attend)


def bwd_kernel(
    width_ref, packed_ref, kvh_ref, starts_ref, qk_ref, mixed_grad_ref,
    out_ref, top_ref, inv_ref,
    joined_ref, dkv_hi_ref, dkvh_ref, k_s, v_s, kt_s, dk_s, dv_s,
):
    for b, rows, k, v in key_blocks(packed_ref, kvh_ref):
        k_s[rows] = k
        v_s[rows] = v
        kt_s[b] = k.T
    dk_s[...] = jnp.zeros_like(dk_s)
    dv_s[...] = jnp.zeros_like(dv_s)

    def attend(block, width):
        first, rows = window_of(block, width)
        q = qk_ref[block, :TOK]
        key = qk_ref[block, TOK:].astype(jnp.float32)
        grad = (mixed_grad_ref[block] * key).astype(jnp.bfloat16)
        grad_t = grad.T
        kt = jnp.concatenate([kt_s[first + n] for n in range(width)], 1)
        scores = masked_scores(k_s[rows], q, starts_ref[block], first, width)
        weights = jnp.exp((scores - top_ref[block]) * SCALE) * inv_ref[block]
        probs = weights.astype(jnp.bfloat16)
        row_dot = jnp.sum(
            out_ref[block].T.astype(jnp.float32) * grad_t.astype(jnp.float32), 0, keepdims=True
        )
        prob_grad = dot_nn(v_s[rows], grad_t)
        score_grad = (weights * (prob_grad - row_dot)).astype(jnp.bfloat16)
        dq = (dot_nn(kt, score_grad) * SCALE).astype(jnp.bfloat16).T
        joined_ref[block, 2 * TOK :] = dq
        dk_s[rows] += dot_nn(score_grad, q)
        dv_s[rows] += dot_nn(probs, grad)

    each_block(width_ref, attend)
    outs = (dkvh_ref, joined_ref, dkv_hi_ref)
    for b in range(SPAN + ROW):
        rows = slice(b * TOK, (b + 1) * TOK)
        ref = outs[b // SPAN]
        ref[b % SPAN, :TOK] = (dk_s[rows] * SCALE).astype(ref.dtype)
        ref[b % SPAN, TOK : 2 * TOK] = dv_s[rows].astype(ref.dtype)


KEYS = (SPAN + ROW) * TOK


def whole(*shape):
    return pl.BlockSpec(shape, lambda b, w: (0,) * len(shape))


VMEM = pl.BlockSpec(memory_space=pltpu.VMEM)


def attention_fwd(widths, packed, kvh, starts, qk):
    operands = [packed, *hbm(kvh), starts, qk]
    return pl.pallas_call(
        fwd_kernel,
        grid_spec=pltpu.PrefetchScalarGridSpec(
            num_scalar_prefetch=1,
            grid=(1,),
            in_specs=[VMEM, whole(SPAN, 2 * TOK, HD), VMEM, VMEM],
            out_specs=[whole(ROW, TOK, HD), whole(ROW, TOK, HD), VMEM, VMEM],
            scratch_shapes=[
                pltpu.VMEM((KEYS, HD), jnp.bfloat16),
                pltpu.VMEM((SPAN + ROW, HD, TOK), jnp.bfloat16),
            ],
        ),
        out_shape=[
            pltpu.HBM((ROW, TOK, HD), jnp.bfloat16),
            pltpu.HBM((ROW, TOK, HD), jnp.bfloat16),
            jax.ShapeDtypeStruct((ROW, 1, TOK), jnp.float32),
            jax.ShapeDtypeStruct((ROW, 1, TOK), jnp.float32),
        ],
        compiler_params=pltpu.CompilerParams(vmem_limit_bytes=20 << 20),
        name="attn_fwd",
    )(widths, *operands)


def attention_bwd(widths, packed, kvh, starts, qk, mixed_grad, out, top, inv):
    operands = [packed, *hbm(kvh), starts, qk, *hbm(mixed_grad, out), top, inv]
    return pl.pallas_call(
        bwd_kernel,
        grid_spec=pltpu.PrefetchScalarGridSpec(
            num_scalar_prefetch=1,
            grid=(1,),
            in_specs=[VMEM, whole(SPAN, 2 * TOK, HD), VMEM, VMEM]
            + [whole(ROW, TOK, HD)] * 2
            + [VMEM] * 2,
            out_specs=[whole(ROW, 3 * TOK, HD), VMEM, VMEM],
            scratch_shapes=[
                pltpu.VMEM((KEYS, HD), jnp.bfloat16),
                pltpu.VMEM((KEYS, HD), jnp.bfloat16),
                pltpu.VMEM((SPAN + ROW, HD, TOK), jnp.bfloat16),
                pltpu.VMEM((KEYS, HD), jnp.float32),
                pltpu.VMEM((KEYS, HD), jnp.float32),
            ],
        ),
        out_shape=[
            pltpu.HBM((ROW, 3 * TOK, HD), jnp.bfloat16),
            jax.ShapeDtypeStruct((SPAN, 2 * TOK, HD), jnp.float32),
            jax.ShapeDtypeStruct((SPAN, 2 * TOK, HD), jnp.bfloat16),
        ],
        compiler_params=pltpu.CompilerParams(vmem_limit_bytes=28 << 20),
        name="attn_bwd",
    )(widths, *operands)


def per_device(
    queries_in, keys_in, values_in, gate_branch, key_branch, mr_filter, out_grad, doc_ids
):
    n_seq = lax.axis_size("seq")
    position = lax.axis_index("seq")
    rings = [list(range(g, g + ROW)) for g in range(0, n_seq, ROW)]

    def swap(x, groups=rings, axis="seq"):
        return lax.all_to_all(x, axis, 0, 0, axis_index_groups=groups, tiled=True)

    def shift(x, by):
        pairs = [(i, i + by) for i in range(n_seq) if 0 <= i + by < n_seq]
        return lax.ppermute(x, "seq", pairs)

    doc_front = jnp.concatenate([jnp.full((SPAN * TOK,), -1, jnp.int32), doc_ids], 0)
    docs = lax.dynamic_slice_in_dim(
        doc_front, (position // ROW) * (ROW * TOK), (SPAN + ROW) * TOK, 0
    ).reshape(SPAN + ROW, TOK)
    widths = jnp.ones((ROW,), jnp.int32)
    for back in range(1, SPAN + 1):
        widths = widths + (docs[SPAN - back : SPAN + ROW - back, -1] == docs[SPAN:, 0])
    numbers = jnp.arange(DOCS, dtype=jnp.int32)[:, None]
    first_rows = jnp.sum((doc_ids[None] < numbers).astype(jnp.int32), 1, keepdims=True)
    first_rows = first_rows - ((position // ROW) * ROW - SPAN) * TOK
    starts = jnp.sum(jnp.where(docs[SPAN:].reshape(1, -1) == numbers, first_rows, 0), 0)
    starts = starts.reshape(ROW, 1, TOK)

    conv_grad = (out_grad.astype(jnp.float32) * gate_branch.astype(jnp.float32)).astype(
        jnp.bfloat16
    )
    grad_edge = shift(conv_grad[:TAPS], -1)
    packed = swap(pack(conv_grad, keys_in, values_in))
    mixed_grad = anti(conv_grad, grad_edge, mr_filter)
    qk = swap(pack(queries_in, key_branch))

    kvh = shift(packed[ROW - SPAN :, TOK:], ROW)
    head_edge = shift(packed[0, :TAPS], -ROW)
    head = position % ROW
    own_taps = lax.dynamic_slice_in_dim(mr_filter, head * HD, HD, 1)
    mixed_grad_head = head_anti(packed, head_edge, own_taps)

    shared = (widths, packed, kvh, starts, qk)
    attn_head, mixed_head, top, inv = attention_fwd(*shared)
    attn_out = swap(attn_head)
    mixed_before = shift(mixed_head[ROW - 1, TOK - TAPS :], ROW)
    joined, dkv_hi, dkvh = attention_bwd(
        *shared, mixed_grad_head, attn_head, top, inv
    )
    back = shift(dkvh, -ROW)
    filter_part = head_corr(mixed_head, mixed_before, packed)
    mixed, branch_grad, last_rows = finish(attn_out, key_branch, mixed_grad)
    mixed_edge = shift(last_rows, 1)
    key_grad, value_grad, query_grad = unpack(swap(join(joined, dkv_hi, back)))
    gate_grad = []
    for piece in range(PIECES):
        gate_grad = [
            causal_piece(piece, mixed, mixed_edge, mr_filter, out_grad, gate_grad)
        ]
    gate_grad = gate_grad[0]

    def partner(x, axis, hop):
        pairs = [(i, i ^ hop) for i in range(lax.axis_size(axis))]
        return lax.ppermute(x, axis, pairs)

    rings_n = n_seq // ROW
    tap_share = TAPS // ROW
    own_filter = lax.dynamic_slice_in_dim(mr_filter, head * tap_share, tap_share, 0)
    filter_grad = filter_part + partner(filter_part, "seq", ROW)
    other = partner(filter_grad, "seq", 2 * ROW)
    filter_grad, norms = norm_parts(filter_grad, other, own_filter)
    hop = 1
    while hop < lax.axis_size("ch"):
        norms = norms + partner(norms, "ch", hop)
        hop *= 2
    tap_rows = TAPS // n_seq
    ring_taps = lax.dynamic_slice_in_dim(
        filter_grad, (position // ROW) * (TAPS // rings_n), TAPS // rings_n, 0
    ).reshape(ROW, tap_rows, HD)
    spread_norms = jnp.broadcast_to(norms[None, :tap_rows], (ROW, tap_rows, HD))
    got = swap(jnp.concatenate([ring_taps, spread_norms], 1))
    filter_step = scaled_step(got, tap_rows)
    return (query_grad, key_grad, value_grad, gate_grad, branch_grad, filter_step)


def solution(mesh):
    rows = P("seq", "ch")
    return jax.shard_map(
        per_device,
        mesh=mesh,
        in_specs=(rows, rows, rows, rows, rows, P(None, "ch"), rows, P()),
        out_specs=(rows,) * 6,
        check_vma=False,
    )
```
